256 devices in a mesh: seq: 32 (over y, z), head: 8 (over x, core).
Axes of the slice: x: 4, y: 4, z: 8, core: 2. Of those that a mesh axis runs over, the one named last changes fastest.
Arguments:
- inputs: bfloat16 [8192, 8192], P('seq'), may hold values from -6 to 6
- w_value: bfloat16 [8192, 4096], P('seq', 'head'), may hold values from -0.0625 to 0.0625
- log_decay: float32 [8192, 64], P('seq', 'head'), may hold values from -1 to 0
- b_proj: bfloat16 [8192, 128], P('seq'), may hold values from -0.5 to 0.5
- c_proj: bfloat16 [8192, 128], P('seq'), may hold values from -0.5 to 0.5
- grad_out: bfloat16 [8192, 4096], P('seq', 'head'), may hold values from -6 to 6
Outputs:
- grad_input: bfloat16 [8192, 8192], P('seq', 'head')
- grad_weight: float32 [8192, 4096], P('seq', 'head')
- grad_b: float32 [8192, 128], P('seq')
- grad_c: float32 [8192, 128], P('seq')
The draws below stay inside these ranges and needn't reach their ends.
All inputs are finite; a program needn't handle non-finite values.
Results may differ from the reference program's by a relative error of at most 0.027.
Values may be sent and summed in bfloat16 or wider, within the bound.
A program may use at most 128 MiB of HBM per device.

```python
import jax
import jax.numpy as jnp
from jax import lax

D = 8192
HEADS = 64
HEAD_DIM = 64
STATE = 128
SPAN = 256
STEPS_DEV = 256
STEPS = 8192
N_SEQ = 32
N_HEAD = 8


def draw_log_decay(key, part):
    keys = [jax.random.fold_in(key, index + 11) for index in range(7)]
    slow_share = 0.5
    slow = jax.random.bernoulli(keys[0], slow_share, (HEADS,))
    slow_rate = jnp.exp(jax.random.uniform(keys[1], (HEADS,), jnp.float32, jnp.log(0.05 / STEPS), jnp.log(1.0 / STEPS)))
    fast_rate = jnp.exp(jax.random.uniform(keys[2], (HEADS,), jnp.float32, jnp.log(1.0 / 50.0), jnp.log(1.0 / 25.0)))
    rate = jnp.where(slow, slow_rate, fast_rate)
    runs = STEPS // STEPS_DEV
    run_factor = jnp.exp(jax.random.uniform(keys[3], (runs, HEADS), jnp.float32, jnp.log(0.5), jnp.log(2.0)))
    run_factor = jnp.repeat(run_factor, STEPS_DEV, axis=0)
    step_factor = jax.random.uniform(keys[4], (STEPS, HEADS), jnp.float32, 0.5, 2.0)
    baseline_offset = -rate[None, :] * step_factor * run_factor
    token_positions = jax.random.randint(keys[5], (3,), 0, STEPS)
    step_numbering = jnp.arange(STEPS, dtype=jnp.int32)
    sudden_spike = jnp.any(step_numbering[:, None] == token_positions[None, :], axis=1)
    damping_level = jax.random.uniform(keys[6], (STEPS, HEADS), jnp.float32, jnp.log(0.5), jnp.log(0.8))
    return (baseline_offset + jnp.where(sudden_spike[:, None], damping_level, 0.0)).astype(jnp.float32)


def spiked(values, stream_key, source, target, parts, factor):
    def block_of(position):
        return (jnp.arange(values.shape[position]) // (values.shape[position] // parts)).reshape((-1,) + (1,) * (values.ndim - 1 - position))

    one_side = jax.random.permutation(stream_key, parts)[block_of(target)]
    second = (block_of(target) + parts // 2) % parts
    return jnp.where((block_of(source) == one_side) | (block_of(source) == second), factor * values, values)


def steps_of(rng, shape, cuts, least, top_value):
    level = 1.0
    for position, parts in cuts:
        heights = jax.random.uniform(jax.random.fold_in(jax.random.fold_in(rng, 6), position), (parts,), jnp.float32, least / len(cuts), top_value / len(cuts))
        level = level * jnp.repeat(jnp.exp(heights), shape[position] // parts).reshape((-1,) + (1,) * (len(shape) - 1 - position))
    return level


def gaussian(key, dims, scale, limit, shards=(), held_as=jnp.bfloat16):
    drawn = scale * jax.random.normal(key, dims, jnp.float32)
    if shards:
        drawn = drawn * steps_of(key, dims, shards, -0.22, 0.18)
    return jnp.clip(drawn, -limit, limit).astype(held_as)


def heavy_noise(rng, shape, spread, most, cuts, heavy, kind=jnp.bfloat16):
    drawn = spread * jax.random.normal(rng, shape, jnp.float32)
    if cuts:
        drawn = drawn * steps_of(rng, shape, cuts, -0.22, 0.18)
    return jnp.clip(spiked(drawn, jax.random.fold_in(rng, 3), *heavy), -most, most).astype(kind)


def setup_inputs(seed: int = 0) -> dict:
    key_list = jax.random.split(jax.random.key(seed), 7)
    return {
        "inputs": heavy_noise(key_list[0], (STEPS, D), 1.0, 6.0, ((0, 32),), (0, 1, 32, 2.75)),
        "w_value": gaussian(key_list[1], (D, HEADS * HEAD_DIM), D ** -0.5, 0.0625, ((0, 32), (1, 8))),
        "log_decay": draw_log_decay(jax.random.fold_in(key_list[6], 71), 0),
        "b_proj": gaussian(key_list[3], (STEPS, STATE), STATE ** -0.5, 0.5, ((0, 32),)),
        "c_proj": gaussian(key_list[4], (STEPS, STATE), STATE ** -0.5, 0.5, ((0, 32),)),
        "grad_out": gaussian(key_list[5], (STEPS, HEADS * HEAD_DIM), 1.0, 6.0, ((0, 32), (1, 8))),
    }


HIGH = lax.Precision.HIGHEST


def block_decay(logs):
    cum_log = jnp.cumsum(logs, axis=0)
    total = cum_log[-1]
    cum_heads = cum_log.T
    rows = lax.broadcasted_iota(jnp.int32, (SPAN, SPAN), 0)
    cols = lax.broadcasted_iota(jnp.int32, (SPAN, SPAN), 1)
    lower = rows >= cols
    diff = cum_heads[:, :, None] - cum_heads[:, None, :]
    decay_mat = jnp.exp(jnp.where(lower[None], diff, -jnp.inf))
    return cum_log, total, decay_mat


def reference(inputs, w_value, log_decay, b_proj, c_proj, grad_out):
    values = jnp.dot(inputs, w_value, preferred_element_type=jnp.float32).astype(jnp.bfloat16)
    blocks = STEPS // SPAN
    xs = values.astype(jnp.float32).reshape(blocks, SPAN, HEADS, HEAD_DIM)
    dys = grad_out.astype(jnp.float32).reshape(blocks, SPAN, HEADS, HEAD_DIM)
    bs = b_proj.astype(jnp.float32).reshape(blocks, SPAN, STATE)
    cs = c_proj.astype(jnp.float32).reshape(blocks, SPAN, STATE)
    logs = log_decay.reshape(blocks, SPAN, HEADS)
    zero_state = jnp.zeros((HEADS, HEAD_DIM, STATE), jnp.float32)

    def forward_step(state, item):
        xk, dyk, bk, ck, lk = item
        cum_log, total, decay_mat = block_decay(lk)
        cross = jnp.einsum("thp,jhp->htj", dyk, xk, precision=HIGH)
        grad_c = jnp.einsum("thp,hpn,th->tn", dyk, state, jnp.exp(cum_log), precision=HIGH)
        grad_c = grad_c + jnp.einsum("htj,jn->tn", decay_mat * cross, bk, precision=HIGH)
        local = jnp.einsum("jhp,jh,jn->hpn", xk, jnp.exp(total[None] - cum_log), bk, precision=HIGH)
        return jnp.exp(total)[:, None, None] * state + local, grad_c

    def backward_step(carried, item):
        xk, dyk, bk, ck, lk = item
        cum_log, total, decay_mat = block_decay(lk)
        shrink = jnp.exp(total[None] - cum_log)
        cross = jnp.einsum("shp,thp->hst", dyk, xk, precision=HIGH)
        scores = jnp.einsum("sn,tn->st", ck, bk, precision=HIGH)
        grad_vals = jnp.einsum("hst,st,shp->thp", decay_mat, scores, dyk, precision=HIGH)
        grad_vals = grad_vals + jnp.einsum("hpn,tn,th->thp", carried, bk, shrink, precision=HIGH)
        grad_b = jnp.einsum("hst,sn->tn", decay_mat * cross, ck, precision=HIGH)
        grad_b = grad_b + jnp.einsum("thp,hpn,th->tn", xk, carried, shrink, precision=HIGH)
        local = jnp.einsum("thp,th,tn->hpn", dyk, jnp.exp(cum_log), ck, precision=HIGH)
        return jnp.exp(total)[:, None, None] * carried + local, (grad_vals, grad_b)

    items = (xs, dys, bs, cs, logs)
    grad_c = lax.scan(forward_step, zero_state, items)[1]
    grad_vals, grad_b = lax.scan(backward_step, zero_state, items, reverse=True)[1]
    grad_values = grad_vals.reshape(STEPS, HEADS * HEAD_DIM).astype(jnp.bfloat16)

    group_cols = HEADS // N_HEAD * HEAD_DIM
    grad_sum = jnp.zeros((STEPS, D), jnp.float32)
    for group in range(N_HEAD):
        part = jnp.dot(grad_values[:, group * group_cols:(group + 1) * group_cols], w_value[:, group * group_cols:(group + 1) * group_cols].T, preferred_element_type=jnp.float32).astype(jnp.bfloat16)
        part = lax.optimization_barrier(part)
        grad_sum = grad_sum + part.astype(jnp.float32)
    grad_input = grad_sum.astype(jnp.bfloat16)

    def add_run(total, item):
        part = jnp.dot(item[0].T, item[1], preferred_element_type=jnp.float32).astype(jnp.bfloat16)
        part = lax.optimization_barrier(part)
        return total + part.astype(jnp.float32), None

    runs = (inputs.reshape(N_SEQ, STEPS_DEV, D), grad_values.reshape(N_SEQ, STEPS_DEV, HEADS * HEAD_DIM))
    grad_weight = lax.scan(add_run, jnp.zeros((D, HEADS * HEAD_DIM), jnp.float32), runs)[0]
    return grad_input, grad_weight, grad_b.reshape(STEPS, STATE), grad_c.reshape(STEPS, STATE)
```

```python
import jax
import jax.numpy as jnp
from jax import lax
from jax.sharding import PartitionSpec as P

SPAN = 256


HIGH = lax.Precision.HIGHEST


def carried_in(array, axis, combine, identity, reverse):
    length, index = (lax.axis_size(axis), lax.axis_index(axis))
    everything = jax.tree.map(
        lambda part, kind: lax.all_gather(part.astype(kind), axis),
        array,
        (jnp.bfloat16, jnp.bfloat16),
    )
    start = jax.tree.map(
        lambda part, zero: jnp.broadcast_to(jnp.asarray(zero, part.dtype), part.shape),
        array,
        identity,
    )

    def lap(k, before):
        at = length - 1 - k if reverse else k
        reached = at > index if reverse else at < index
        new = combine(
            before, jax.tree.map(lambda part, own: part[at].astype(own.dtype), everything, array)
        )
        return jax.tree.map(lambda a, b: jnp.where(reached, a, b), new, before)

    return lax.fori_loop(0, length, lap, start)


def link(earlier, later):
    return (earlier[0] * later[0], later[0][:, None, None] * earlier[1] + later[1])


def advance_once(carried, item):
    decay, local = item
    return (decay[:, None, None] * carried + local, carried)


def per_device(inputs, w_value, log_decay, b_proj, c_proj, grad_out):
    steps = inputs.shape[0]
    heads = log_decay.shape[1]
    columns = grad_out.shape[1]
    depth = columns // heads
    states = b_proj.shape[1]
    blocks = steps // SPAN
    w_full = lax.all_gather(w_value, "seq", axis=0, tiled=True)
    values = jnp.dot(inputs, w_full, preferred_element_type=jnp.float32).astype(jnp.bfloat16)
    xs = values.astype(jnp.float32).reshape(blocks, SPAN, heads, depth)
    dys = grad_out.astype(jnp.float32).reshape(blocks, SPAN, heads, depth)
    bs = b_proj.astype(jnp.float32).reshape(blocks, SPAN, states)
    cs = c_proj.astype(jnp.float32).reshape(blocks, SPAN, states)
    before_or_at = jnp.tril(jnp.ones((SPAN, SPAN), jnp.float32))
    cum_log = jnp.einsum(
        "tj,kjh->kth", before_or_at, log_decay.reshape(blocks, SPAN, heads), precision=HIGH
    )
    totals = cum_log[:, -1]
    grow = jnp.exp(cum_log)
    shrink = jnp.exp(totals[:, None] - cum_log)
    cum_heads = jnp.swapaxes(cum_log, 1, 2)
    rows = lax.broadcasted_iota(jnp.int32, (SPAN, SPAN), 0)
    cols = lax.broadcasted_iota(jnp.int32, (SPAN, SPAN), 1)
    lower = (rows >= cols)[None, None]
    diff = cum_heads[:, :, :, None] - cum_heads[:, :, None, :]
    decay_mat = jnp.exp(jnp.where(lower, diff, -jnp.inf))
    cross = jnp.einsum("kthp,kjhp->khtj", dys, xs, precision=HIGH)
    mixed = decay_mat * cross
    scores = jnp.einsum("ktn,kjn->ktj", cs, bs, precision=HIGH)
    span_decay = jnp.exp(totals)
    dev_decay = jnp.exp(jnp.sum(totals, axis=0))
    zero_state = jnp.zeros((heads, depth, states), jnp.float32)
    identity_matrix = (jnp.ones_like(dev_decay), zero_state)
    local_end = jnp.einsum("kjhp,kjh,kjn->khpn", xs, shrink, bs, precision=HIGH)
    dev_state, before = lax.scan(advance_once, zero_state, (span_decay, local_end))
    incoming = carried_in((dev_decay, dev_state), "seq", link, identity_matrix, False)[1]
    earlier = jnp.tril(jnp.ones((blocks, blocks), jnp.float32))
    through = jnp.einsum("kl,lh->kh", earlier, totals, precision=HIGH)
    lead = jnp.exp(through - totals)
    state_in = before + lead[:, :, None, None] * incoming[None]
    grad_c = jnp.einsum("kthp,khpn,kth->ktn", dys, state_in, grow, precision=HIGH)
    grad_c = grad_c + jnp.einsum("khtj,kjn->ktn", mixed, bs, precision=HIGH)
    local_back = jnp.einsum("kthp,kth,ktn->khpn", dys, grow, cs, precision=HIGH)
    dev_back, after = lax.scan(advance_once, zero_state, (span_decay, local_back), reverse=True)
    incoming_back = carried_in((dev_decay, dev_back), "seq", link, identity_matrix, True)[1]
    trail = jnp.exp(jnp.sum(totals, axis=0)[None] - through)
    grad_in = after + trail[:, :, None, None] * incoming_back[None]
    grad_vals = jnp.einsum("khst,kst,kshp->kthp", decay_mat, scores, dys, precision=HIGH)
    grad_vals = grad_vals + jnp.einsum("khpn,ktn,kth->kthp", grad_in, bs, shrink, precision=HIGH)
    grad_b = jnp.einsum("khst,ksn->ktn", mixed, cs, precision=HIGH)
    grad_b = grad_b + jnp.einsum("kthp,khpn,kth->ktn", xs, grad_in, shrink, precision=HIGH)
    grad_values = grad_vals.reshape(steps, columns).astype(jnp.bfloat16)
    grad_b, grad_c = (
        lax.psum(grad_b.reshape(steps, states).astype(jnp.bfloat16), "head").astype(jnp.float32),
        lax.psum(grad_c.reshape(steps, states).astype(jnp.bfloat16), "head").astype(jnp.float32),
    )
    term = lax.dot_general(
        grad_values, w_full, (((1,), (1,)), ((), ())), preferred_element_type=jnp.float32
    )
    grad_input = lax.psum_scatter(
        term.astype(jnp.bfloat16), "head", scatter_dimension=1, tiled=True
    )
    grad_weight = lax.psum_scatter(
        lax.dot_general(
            inputs, grad_values, (((0,), (0,)), ((), ())), preferred_element_type=jnp.float32
        ).astype(jnp.bfloat16),
        "seq",
        scatter_dimension=0,
        tiled=True,
    ).astype(jnp.float32)
    return (grad_input, grad_weight, grad_b, grad_c)


def solution(mesh):
    placed = (
        P("seq", None),
        P("seq", "head"),
        P("seq", "head"),
        P("seq", None),
        P("seq", None),
        P("seq", "head"),
    )
    return jax.shard_map(
        per_device,
        mesh=mesh,
        in_specs=placed,
        out_specs=(P("seq", "head"), P("seq", "head"), P("seq", None), P("seq", None)),
        check_vma=False,
    )
```

```python
import jax
import jax.numpy as jnp
from jax import lax
from jax.experimental import pallas as pl
from jax.experimental.pallas import tpu as pltpu
from jax.sharding import Mesh
from jax.sharding import PartitionSpec as P

NY, NZ, NX, NC = 4, 8, 4, 2
RUN = 256
HALF = RUN // 2
COLS = 512
HEADS = 8
DEPTH = 64
STATES = 128
QUARTER = 2048
SLICE = 1024
PACK = DEPTH + 32
F32, BF16 = jnp.float32, jnp.bfloat16
HIGH = lax.Precision.HIGHEST

M_W = 0
M_WS = M_W + 16
M_X = M_WS + 1
M_XS = M_X + 3
M_BACK = M_XS + 3
M_FORE = M_BACK + 17
M_G = M_FORE + 17
M_GS = M_G + 3
M_V = M_GS + 4
M_GW = M_V + 6
M_GI = M_GW + 16
M_T = M_GI + 6
M_S = M_T + 2
MESSAGES = M_S + 5


def dot(a, b, dims=((1,), (0,)), precision=None):
    return lax.dot_general(a, b, (dims, ((), ())), preferred_element_type=F32, precision=precision)


def kernel(
    x_hbm, w_ref, log_ref, b_ref, c_ref, dy_ref,
    gi_ref, gw_ref, gb_ref, gc_ref,
    wq, ws, xq, gq, gs, dec, gvi, grow_x, shrink_x, dg, xs, vals, gin, hin,
    b1, r1, b2, r2, b3, r3, f1, p1, f2, p2, f3, p3,
    acc, vs, vr, gws, gwr, gis, gir, gi_sum, gi_fin,
    sib_send, sib_recv, red, tot_send, tot_recv,
    send_sem, recv_sem, local_sem,
):
    y, z = lax.axis_index("y"), lax.axis_index("z")
    x, core = lax.axis_index("x"), lax.axis_index("core")
    other = 1 - core
    pending = []

    def message(src, dst, index, **to):
        return pltpu.make_async_remote_copy(
            src_ref=src, dst_ref=dst, send_sem=send_sem.at[index], recv_sem=recv_sem.at[index],
            device_id=to, device_id_type=pl.DeviceIdType.MESH,
        )

    def send(src, dst, index, **to):
        copy = message(src, dst, index, **to)
        copy.start()
        pending.append(copy)

    def arrived(dst, index, **to):
        message(dst, dst, index, **to).wait_recv()

    def rows(ref, start, size):
        return ref.at[pl.ds(pl.multiple_of(start, size), size), :]

    barrier = pltpu.get_barrier_semaphore()
    for d in range(1, NZ):
        pl.semaphore_signal(barrier, inc=1, device_id={"z": lax.rem(z + d, NZ)}, device_id_type=pl.DeviceIdType.MESH)
    for d in range(1, NY):
        pl.semaphore_signal(barrier, inc=1, device_id={"y": lax.rem(y + d, NY)}, device_id_type=pl.DeviceIdType.MESH)
    for d in range(1, NX):
        pl.semaphore_signal(barrier, inc=1, device_id={"x": lax.rem(x + d, NX)}, device_id_type=pl.DeviceIdType.MESH)
    pl.semaphore_signal(barrier, inc=1, device_id={"core": other}, device_id_type=pl.DeviceIdType.MESH)

    @pl.when(x != y)
    def _():
        pl.semaphore_signal(barrier, inc=1, device_id={"x": y, "y": x}, device_id_type=pl.DeviceIdType.MESH)

    own_x = pltpu.make_async_copy(
        x_hbm.at[:, pl.ds(pl.multiple_of(y * QUARTER, QUARTER), QUARTER)], rows(xq, y * RUN, RUN), local_sem
    )
    own_x.start()
    wq[pl.ds(pl.multiple_of(z * RUN, RUN), RUN), :] = w_ref[...]

    @pl.when(x == y)
    def _():
        pl.semaphore_wait(barrier, NZ + NY + NX - 2)

    @pl.when(x != y)
    def _():
        pl.semaphore_wait(barrier, NZ + NY + NX - 1)

    ring_z = (lax.rem(z + 1, NZ), lax.rem(z + NZ - 1, NZ))

    def w_part(shard, half):
        return rows(wq, shard * RUN + half * HALF, HALF)

    def w_send(way, hop, half):
        shard = lax.rem(z + NZ - (hop - 1), NZ) if way == 0 else lax.rem(z + (hop - 1), NZ)
        send(w_part(shard, half), w_part(shard, half), M_W + way * 8 + (hop - 1) * 2 + half, z=ring_z[way])

    def w_step(hop):
        for half in (0, 1):
            for way in (0, 1):
                if hop == NZ // 2 and half != way:
                    continue
                shard = lax.rem(z + NZ - hop, NZ) if way == 0 else lax.rem(z + hop, NZ)
                arrived(w_part(shard, half), M_W + way * 8 + (hop - 1) * 2 + half, z=ring_z[way])
                if hop < NZ // 2 - 1 or (hop == NZ // 2 - 1 and half == way):
                    w_send(way, hop + 1, half)

    for half in (0, 1):
        for way in (0, 1):
            w_send(way, 1, half)

    def x_part(row, col):
        return xq.at[
            pl.ds(pl.multiple_of(row * RUN, RUN), RUN), pl.ds(pl.multiple_of(col * SLICE, SLICE), SLICE)
        ]

    for d in (2, 1, 3):
        to = lax.rem(y + d, NY)
        send(
            x_hbm.at[:, pl.ds(pl.multiple_of(to * QUARTER + core * SLICE, SLICE), SLICE)],
            x_part(y, core), M_X + d - 1, y=to,
        )

    one = lax.broadcasted_iota(jnp.int32, (RUN, RUN), 0)
    two = lax.broadcasted_iota(jnp.int32, (RUN, RUN), 1)
    logs = log_ref[...]
    cum = dot((one >= two).astype(F32), logs, precision=HIGH)
    cum_t = dot(logs, (one <= two).astype(F32), ((0,), (0,)), HIGH)
    head_of = lax.broadcasted_iota(jnp.int32, (HEADS, COLS), 1) // DEPTH
    spread = (lax.broadcasted_iota(jnp.int32, (HEADS, COLS), 0) == head_of).astype(F32)
    cum_x = dot(cum, spread, precision=HIGH)
    grow_x[...] = jnp.exp(cum_x)
    shrink_x[...] = jnp.exp(cum_x[RUN - 1 :, :] - cum_x)
    dg[...] = (dy_ref[...].astype(F32) * grow_x[...]).astype(BF16)

    def scan_out(states, sent, got, base):
        for k in range(HEADS):
            sent[k, :DEPTH, :] = states[k * DEPTH : (k + 1) * DEPTH].astype(BF16)
            decay = jnp.exp(jnp.broadcast_to(cum[RUN - 1 :, k : k + 1], (16, STATES)))
            high = decay.astype(BF16)
            sent[k, DEPTH : DEPTH + 16, :] = high
            sent[k, DEPTH + 16 :, :] = (decay - high.astype(F32)).astype(BF16)
        for d in range(1, NZ):
            to = lax.rem(z + d, NZ)
            send(sent.at[to], got.at[z], base + d - 1, z=to)
        got[pl.ds(z, 1)] = sent[pl.ds(z, 1)]

    def unpack(ref, k):
        decay = ref[k, DEPTH : DEPTH + 16, :].astype(F32) + ref[k, DEPTH + 16 :, :].astype(F32)
        return ref[k, :DEPTH, :].astype(F32), decay[:1, :]

    def scan_rows(got, sent, got_y, base, order):
        for d in range(1, NZ):
            arrived(got.at[lax.rem(z + NZ - d, NZ)], base + d - 1, z=ring_z[0])
        carried, decays = jnp.zeros((DEPTH, STATES), F32), jnp.ones((1, STATES), F32)
        for k in order:
            state, decay = unpack(got, k)
            carried = decay * carried + state
            decays = decays * decay
        decays = jnp.broadcast_to(decays, (16, STATES))
        high = decays.astype(BF16)
        sent[:DEPTH, :] = carried.astype(BF16)
        sent[DEPTH : DEPTH + 16, :] = high
        sent[DEPTH + 16 :, :] = (decays - high.astype(F32)).astype(BF16)
        for d in range(1, NY):
            to = lax.rem(y + d, NY)
            send(sent, got_y.at[y], base + 7 + d - 1, y=to)
        got_y[pl.ds(y, 1)] = sent[...][None]

    def scan_back(got, got_y, sent, got_z, base, order, reverse):
        for d in range(1, NY):
            arrived(got_y.at[lax.rem(y + NY - d, NY)], base + 7 + d - 1, y=lax.rem(y + 1, NY))
        carried = jnp.zeros((DEPTH, STATES), F32)
        for k in reversed(range(NY)) if reverse else range(NY):
            state, decay = unpack(got_y, k)
            reached = (y < k) if reverse else (y > k)
            carried = jnp.where(reached, decay * carried + state, carried)
        for k in order:
            sent[k] = carried.astype(BF16)
            state, decay = unpack(got, k)
            carried = decay * carried + state
        for d in range(1, NZ):
            to = lax.rem(z + d, NZ)
            send(sent.at[to], got_z.at[z], base + 10 + d - 1, z=to)
        got_z[pl.ds(z, 1)] = sent[pl.ds(z, 1)]

    def scan_in(got_z, base, into):
        for d in range(1, NZ):
            arrived(got_z.at[lax.rem(z + NZ - d, NZ)], base + 10 + d - 1, z=ring_z[0])
        for k in range(HEADS):
            into[k * DEPTH : (k + 1) * DEPTH, :] = got_z[k]

    scan_out(dot(dg[...], c_ref[...], ((0,), (0,))), b1, r1, M_BACK)
    down, up = tuple(reversed(range(NZ))), tuple(range(NZ))

    scores = dot(b_ref[...], c_ref[...], ((1,), (1,)))
    low = lax.broadcasted_iota(jnp.int32, (RUN, 2 * DEPTH), 1) < DEPTH

    def within(pair):
        columns = slice(pair * 2 * DEPTH, (pair + 1) * 2 * DEPTH)
        part = dy_ref[:, columns]
        total = jnp.zeros((RUN, 2 * DEPTH), F32)
        for side in (0, 1):
            h = 2 * pair + side
            between = cum_t[h : h + 1, :] - cum[:, h : h + 1]
            decay = jnp.exp(jnp.where(two >= one, between, -1e30))
            dec[h] = decay
            kept = jnp.where(low if side == 0 else ~low, part, jnp.zeros_like(part))
            total = total + dot((decay * scores).astype(BF16), kept)
        gvi[:, columns] = total

    within(0)
    within(1)
    w_step(1)
    scan_rows(r1, b2, r2, M_BACK, down)
    within(2)
    within(3)
    w_step(2)
    scan_back(r1, r2, b3, r3, M_BACK, down, True)
    w_step(3)
    scan_in(r3, M_BACK, gin)

    def g_part(ref, row):
        return rows(ref, row * RUN, RUN)

    grad_values = gvi[...] + dot(b_ref[...], gin[...], ((1,), (1,))) * shrink_x[...]
    gq[pl.ds(pl.multiple_of(y * RUN, RUN), RUN), :] = grad_values.astype(BF16)
    for d in (2, 1, 3):
        send(g_part(gq, y), g_part(gq, y), M_G + d - 1, y=lax.rem(y + d, NY))
    send(g_part(gq, y), g_part(gs, y), M_GS, core=other)

    w_step(4)
    theirs = pl.multiple_of(other * SLICE, SLICE)
    mine = pl.multiple_of(core * SLICE, SLICE)
    send(wq.at[pl.ds(theirs, SLICE), :], ws, M_WS, core=other)
    for d in (1, 3, 2):
        part = x_part(lax.rem(y + NY - d, NY), core)
        arrived(part, M_X + d - 1, y=lax.rem(y + 1, NY))
        send(part, part, M_XS + d - 1, core=other)
    own_x.wait()
    for d in (1, 3, 2):
        source = lax.rem(y + NY - d, NY)
        arrived(g_part(gq, source), M_G + d - 1, y=lax.rem(y + 1, NY))
        send(g_part(gq, source), g_part(gs, source), M_GS + d, core=other)

    for d in range(1, NY):
        arrived(x_part(lax.rem(y + NY - d, NY), other), M_XS + d - 1, core=other)

    def gw_own(dest):
        columns = pl.ds(pl.multiple_of(dest * RUN, RUN), RUN)
        return dot(xq[:, columns], gq[...], ((0,), (0,)))

    def gw_step(t):
        for way in (0, 1):
            dest = lax.rem(z + 4 - t, NZ) if way == 0 else lax.rem(z + 4 + t, NZ)
            own = gw_own(dest)
            for half in (way, 1 - way):
                if t == 0 and half != way:
                    continue
                part = own[half * HALF : (half + 1) * HALF]
                index = way * 8 + t * 2 + half
                if t > 1 or (t == 1 and half == way):
                    arrived(gwr.at[way, t - 1, half], M_GW + index - 2, z=ring_z[way])
                    part = part + gwr[way, t - 1, half].astype(F32)
                gws[way, t, half] = part.astype(BF16)
                send(gws.at[way, t, half], gwr.at[way, t, half], M_GW + index, z=ring_z[way])

    def gw_end():
        own = gw_own(z)
        for half in (0, 1):
            part = own[half * HALF : (half + 1) * HALF]
            for way in (0, 1):
                arrived(gwr.at[way, 3, half], M_GW + way * 8 + 6 + half, z=ring_z[way])
                part = part + gwr[way, 3, half].astype(F32)
            gw_ref[half * HALF : (half + 1) * HALF, :] = part

    def four_step(t, axis, me, own, sent, got, base):
        ends = []
        for way in (0, 1):
            dest = lax.rem(me + 3 - t, 4) if way == 0 else lax.rem(me + 1 + t, 4)
            to = lax.rem(me + 1, 4) if way == 0 else lax.rem(me + 3, 4)
            part = own(dest, way)
            if t > 0:
                arrived(got.at[way, t - 1], base + way * 3 + t - 1, **{axis: to})
                part = part + got[way, t - 1].astype(F32)
            if t < 3:
                sent[way, t] = part.astype(BF16)
                send(sent.at[way, t], got.at[way, t], base + way * 3 + t, **{axis: to})
            ends.append(part)
        return ends

    def gi_own(dest, half):
        block = pl.ds(pl.multiple_of(dest * RUN + half * HALF, HALF), HALF)
        return dot(gq[block, :], wq[pl.ds(mine, SLICE), :], ((1,), (1,))) + dot(gs[block, :], ws[...], ((1,), (1,)))

    def gi_step(t):
        return four_step(t, "x", x, gi_own, gis, gir, M_GI)

    gw_step(0)
    arrived(ws, M_WS, core=other)
    for d in range(NY):
        arrived(g_part(gs, lax.rem(y + NY - d, NY)), M_GS + d, core=other)
    gi_step(0)

    def product(k, _):
        block = pl.ds(pl.multiple_of(k * RUN, RUN), RUN)
        acc[block, :] = dot(xq[block, :], wq[...])
        return 0

    lax.fori_loop(0, NY, product, 0)

    def v_own(dest, half):
        return acc[pl.ds(pl.multiple_of(dest * RUN + half * HALF, HALF), HALF), :]

    def v_step(t):
        return four_step(t, "y", y, v_own, vs, vr, M_V)

    v_step(0)
    gw_step(1)
    v_step(1)
    gi_step(1)
    v_step(2)
    gw_step(2)
    for half, part in enumerate(v_step(3)):
        vals[half * HALF : (half + 1) * HALF, :] = part.astype(BF16)
    xs[...] = (vals[...].astype(F32) * shrink_x[...]).astype(BF16)
    scan_out(dot(xs[...], b_ref[...], ((0,), (0,))), f1, p1, M_FORE)
    gi_step(2)
    gw_step(3)
    scan_rows(p1, f2, p2, M_FORE, up)

    mixed = jnp.zeros((RUN, RUN), F32)
    for pair in range(HEADS // 2):
        columns = slice(pair * 2 * DEPTH, (pair + 1) * 2 * DEPTH)
        part = vals[:, columns]
        for side in (0, 1):
            kept = jnp.where(low if side == 0 else ~low, part, jnp.zeros_like(part))
            mixed = mixed + dec[2 * pair + side] * dot(kept, dy_ref[:, columns], ((1,), (1,)))
    mixed = mixed.astype(BF16)
    grad_b = dot(mixed, c_ref[...]) + dot(xs[...], gin[...])
    grad_c = dot(mixed, b_ref[...], ((0,), (0,)))
    scan_back(p1, p2, f3, p3, M_FORE, up, False)

    for half, part in enumerate(gi_step(3)):
        gi_sum[half * HALF : (half + 1) * HALF, :] = part.astype(BF16)

        @pl.when(x != y)
        def _(half=half):
            block = pl.ds(half * HALF, HALF)
            message(gi_sum.at[block, :], gi_fin.at[block, :], M_T + half, x=y, y=x).start()

    scan_in(p3, M_FORE, hin)
    grad_c = grad_c + dot(dg[...], hin[...])

    sib_send[...] = jnp.where(core == 0, grad_c, grad_b)
    send(sib_send, sib_recv, M_S, core=other)
    arrived(sib_recv, M_S, core=other)
    red[pl.ds(x, 1)] = (jnp.where(core == 0, grad_b, grad_c) + sib_recv[...]).astype(BF16)[None]
    for d in range(1, NX):
        send(red.at[x], red.at[x], M_S + d, x=lax.rem(x + d, NX))
    gw_end()
    for d in range(1, NX):
        arrived(red.at[lax.rem(x + NX - d, NX)], M_S + d, x=lax.rem(x + 1, NX))
    total = red[0].astype(F32)
    for k in range(1, NX):
        total = total + red[k].astype(F32)
    tot_send[...] = total
    send(tot_send, tot_recv, M_S + 4, core=other)
    arrived(tot_recv, M_S + 4, core=other)
    gb_ref[...] = jnp.where(core == 0, tot_send[...], tot_recv[...])
    gc_ref[...] = jnp.where(core == 0, tot_recv[...], tot_send[...])

    @pl.when(x != y)
    def _():
        for half in (0, 1):
            block = pl.ds(half * HALF, HALF)
            copy = message(gi_sum.at[block, :], gi_fin.at[block, :], M_T + half, x=y, y=x)
            copy.wait_send()
            copy.wait_recv()
        gi_ref[...] = gi_fin[...]

    @pl.when(x == y)
    def _():
        gi_ref[...] = gi_sum[...]

    for copy in pending:
        copy.wait_send()


def per_device(inputs, w_value, log_decay, b_proj, c_proj, grad_out):
    vmem = pl.BlockSpec(memory_space=pltpu.VMEM)

    def pair(count, *rest):
        return [pltpu.VMEM((count, *rest), BF16)] * 2

    scan = [
        *pair(HEADS, PACK, STATES),
        pltpu.VMEM((PACK, STATES), BF16),
        pltpu.VMEM((NY, PACK, STATES), BF16),
        *pair(HEADS, DEPTH, STATES),
    ]
    return pl.pallas_call(
        kernel,
        out_shape=(
            jax.ShapeDtypeStruct((RUN, SLICE), BF16),
            jax.ShapeDtypeStruct((RUN, COLS), F32),
            jax.ShapeDtypeStruct((RUN, STATES), F32),
            jax.ShapeDtypeStruct((RUN, STATES), F32),
        ),
        in_specs=[pl.BlockSpec(memory_space=pl.ANY), vmem, vmem, vmem, vmem, vmem],
        out_specs=(vmem, vmem, vmem, vmem),
        scratch_shapes=[
            pltpu.VMEM((QUARTER, COLS), BF16),
            pltpu.VMEM((SLICE, COLS), BF16),
            pltpu.VMEM((NY * RUN, QUARTER), BF16),
            pltpu.VMEM((NY * RUN, COLS), BF16),
            pltpu.VMEM((NY * RUN, COLS), BF16),
            pltpu.VMEM((HEADS, RUN, RUN), F32),
            pltpu.VMEM((RUN, COLS), F32),
            pltpu.VMEM((RUN, COLS), F32),
            pltpu.VMEM((RUN, COLS), F32),
            pltpu.VMEM((RUN, COLS), BF16),
            pltpu.VMEM((RUN, COLS), BF16),
            pltpu.VMEM((RUN, COLS), BF16),
            pltpu.VMEM((HEADS * DEPTH, STATES), BF16),
            pltpu.VMEM((HEADS * DEPTH, STATES), BF16),
            *scan,
            *scan,
            pltpu.VMEM((NY * RUN, COLS), F32),
            *pair(2, 3, HALF, COLS),
            *pair(2, 4, 2, HALF, COLS),
            *pair(2, 3, HALF, SLICE),
            *pair(RUN, SLICE),
            pltpu.VMEM((RUN, STATES), F32),
            pltpu.VMEM((RUN, STATES), F32),
            pltpu.VMEM((NX, RUN, STATES), BF16),
            pltpu.VMEM((RUN, STATES), F32),
            pltpu.VMEM((RUN, STATES), F32),
            pltpu.SemaphoreType.DMA((MESSAGES,)),
            pltpu.SemaphoreType.DMA((MESSAGES,)),
            pltpu.SemaphoreType.DMA,
        ],
        compiler_params=pltpu.CompilerParams(
            collective_id=0, has_side_effects=True, vmem_limit_bytes=56 * 2**20
        ),
        name="ssd_backward",
    )(inputs, w_value, log_decay, b_proj, c_proj, grad_out)


def solution(mesh):
    grid = Mesh(mesh.devices.reshape(NY, NZ, NX, NC), ("y", "z", "x", "core"))
    seq, head = ("y", "z"), ("x", "core")
    placed = (P(seq, None), P(seq, head), P(seq, head), P(seq, None), P(seq, None), P(seq, head))
    return jax.shard_map(
        per_device,
        mesh=grid,
        in_specs=placed,
        out_specs=(P(seq, head), P(seq, head), P(seq, None), P(seq, None)),
        check_vma=False,
    )
```

```python
import jax
import jax.numpy as jnp
from jax import lax
from jax.experimental import pallas as pl
from jax.experimental.pallas import tpu as pltpu
from jax.sharding import Mesh
from jax.sharding import PartitionSpec as P

NY, NZ, NX, NC = 4, 8, 4, 2
RUN = 256
HALF = RUN // 2
COLS = 512
HEADS = 8
DEPTH = 64
STATES = 128
QUARTER = 2048
SLICE = 1024
SUB = 256
PIECE = 64
PACK = DEPTH + 32
F32, BF16 = jnp.float32, jnp.bfloat16
HIGH = lax.Precision.HIGHEST

M_W = 0
M_WS = M_W + 16
M_X = M_WS + 1
M_XX = M_X + 3
M_XS = M_XX + 9
M_BACK = M_XS + 3
M_FORE = M_BACK + 17
M_G = M_FORE + 17
M_GS = M_G + 3
M_V = M_GS + 4
M_GW = M_V + 6
M_C = M_GW + 16
M_D = M_C + 16
M_S = M_D + 4
MESSAGES = M_S + 5


def dot(a, b, dims=((1,), (0,)), precision=None):
    return lax.dot_general(a, b, (dims, ((), ())), preferred_element_type=F32, precision=precision)


def kernel(
    x_hbm, w_ref, log_t_ref, b_ref, c_ref, dy_ref,
    gi_ref, gw_ref, gb_ref, gc_ref,
    wq, ws, xq, gq, gs, dec, gvi, grow_x, shrink_x, dg, xs, vals, gin, hin,
    b1, r1, b2, r2, b3, r3, f1, p1, f2, p2, f3, p3,
    acc, gia, vs, vr, gws, gwr, gis, gir, gi_fin,
    sib_send, sib_recv, red, tot_send, tot_recv,
    send_sem, recv_sem, local_sem,
):
    y, z = lax.axis_index("y"), lax.axis_index("z")
    x, core = lax.axis_index("x"), lax.axis_index("core")
    other = 1 - core
    pending = []

    def message(src, dst, index, at=None, **to):
        return pltpu.make_async_remote_copy(
            src_ref=src, dst_ref=dst, send_sem=send_sem.at[index], recv_sem=recv_sem.at[index if at is None else at],
            device_id=to, device_id_type=pl.DeviceIdType.MESH,
        )

    def send(src, dst, index, **to):
        copy = message(src, dst, index, **to)
        copy.start()
        pending.append(copy)

    def arrived(dst, index, **to):
        message(dst, dst, index, **to).wait_recv()

    def rows(ref, start, size):
        return ref.at[pl.ds(pl.multiple_of(start, size), size), :]

    barrier = pltpu.get_barrier_semaphore()
    for d in range(1, NZ):
        pl.semaphore_signal(barrier, inc=1, device_id={"z": lax.rem(z + d, NZ)}, device_id_type=pl.DeviceIdType.MESH)
    for d in range(1, NY):
        pl.semaphore_signal(barrier, inc=1, device_id={"y": lax.rem(y + d, NY)}, device_id_type=pl.DeviceIdType.MESH)
    for d in range(1, NX):
        pl.semaphore_signal(barrier, inc=1, device_id={"x": lax.rem(x + d, NX)}, device_id_type=pl.DeviceIdType.MESH)
    pl.semaphore_signal(barrier, inc=1, device_id={"core": other}, device_id_type=pl.DeviceIdType.MESH)

    own_x = pltpu.make_async_copy(
        x_hbm.at[:, pl.ds(pl.multiple_of(y * QUARTER, QUARTER), QUARTER)], rows(xq, y * RUN, RUN), local_sem
    )
    own_x.start()
    wq[pl.ds(pl.multiple_of(z * RUN, RUN), RUN), :] = w_ref[...]

    one = lax.broadcasted_iota(jnp.int32, (RUN, RUN), 0)
    two = lax.broadcasted_iota(jnp.int32, (RUN, RUN), 1)
    logs = log_t_ref[...]
    cum = dot((one >= two).astype(F32), logs, ((1,), (1,)), HIGH)
    cum_t = dot(logs, (one <= two).astype(F32), precision=HIGH)
    head_of = lax.broadcasted_iota(jnp.int32, (HEADS, COLS), 1) // DEPTH
    spread = (lax.broadcasted_iota(jnp.int32, (HEADS, COLS), 0) == head_of).astype(F32)
    cum_x = dot(cum, spread, precision=HIGH)
    grow_x[...] = jnp.exp(cum_x)
    shrink_x[...] = jnp.exp(cum_x[RUN - 1 :, :] - cum_x)
    dg[...] = (dy_ref[...].astype(F32) * grow_x[...]).astype(BF16)

    def scan_pack(states, sent):
        for k in range(HEADS):
            sent[k, :DEPTH, :] = states[k * DEPTH : (k + 1) * DEPTH].astype(BF16)
            decay = jnp.exp(jnp.broadcast_to(cum[RUN - 1 :, k : k + 1], (16, STATES)))
            high = decay.astype(BF16)
            sent[k, DEPTH : DEPTH + 16, :] = high
            sent[k, DEPTH + 16 :, :] = (decay - high.astype(F32)).astype(BF16)

    def scan_out(sent, got, base):
        for d in (4, 3, 5, 2, 6, 1, 7):
            to = lax.rem(z + d, NZ)
            send(sent.at[to], got.at[z], base + d - 1, z=to)
        got[pl.ds(z, 1)] = sent[pl.ds(z, 1)]

    scan_pack(dot(dg[...], c_ref[...], ((0,), (0,))), b1)
    pl.semaphore_wait(barrier, NZ + NY + NX - 2)
    scan_out(b1, r1, M_BACK)

    ring_z = (lax.rem(z + 1, NZ), lax.rem(z + NZ - 1, NZ))

    def w_part(shard, half):
        return rows(wq, shard * RUN + half * HALF, HALF)

    def w_send(way, hop, half):
        shard = lax.rem(z + NZ - (hop - 1), NZ) if way == 0 else lax.rem(z + (hop - 1), NZ)
        send(w_part(shard, half), w_part(shard, half), M_W + way * 8 + (hop - 1) * 2 + half, z=ring_z[way])

    def w_step(hop):
        for half in (0, 1):
            for way in (0, 1):
                if hop == NZ // 2 and half != way:
                    continue
                shard = lax.rem(z + NZ - hop, NZ) if way == 0 else lax.rem(z + hop, NZ)
                arrived(w_part(shard, half), M_W + way * 8 + (hop - 1) * 2 + half, z=ring_z[way])
                if hop < NZ // 2 - 1 or (hop == NZ // 2 - 1 and half == way):
                    w_send(way, hop + 1, half)

    for half in (0, 1):
        for way in (0, 1):
            w_send(way, 1, half)

    def x_part(row, col):
        return xq.at[
            pl.ds(pl.multiple_of(row * RUN, RUN), RUN), pl.ds(pl.multiple_of(col * SLICE, SLICE), SLICE)
        ]

    def x_piece(row, sub):
        return xq.at[
            pl.ds(pl.multiple_of(row * RUN, RUN), RUN), pl.ds(pl.multiple_of(core * SLICE + sub * SUB, SUB), SUB)
        ]

    for d in (2, 1, 3):
        to = lax.rem(y + d, NY)
        columns = pl.ds(pl.multiple_of(to * QUARTER + core * SLICE + x * SUB, SUB), SUB)
        send(x_hbm.at[:, columns], x_piece(y, x), M_X + d - 1, y=to)

    def x_relay():
        for d in (1, 3, 2):
            source = lax.rem(y + NY - d, NY)
            arrived(x_piece(source, x), M_X + d - 1, y=lax.rem(y + 1, NY))
            for e in (2, 1, 3):
                send(x_piece(source, x), x_piece(source, x), M_XX + (d - 1) * 3 + e - 1, x=lax.rem(x + e, NX))

    def x_collect():
        for d in (1, 3, 2):
            source = lax.rem(y + NY - d, NY)
            for e in (1, 2, 3):
                arrived(x_piece(source, lax.rem(x + NX - e, NX)), M_XX + (d - 1) * 3 + e - 1, x=lax.rem(x + 1, NX))
            send(x_part(source, core), x_part(source, core), M_XS + d - 1, core=other)

    def unpack(ref, k):
        decay = ref[k, DEPTH : DEPTH + 16, :].astype(F32) + ref[k, DEPTH + 16 :, :].astype(F32)
        return ref[k, :DEPTH, :].astype(F32), decay[:1, :]

    def scan_rows(got, sent, got_y, base, order):
        for d in range(1, NZ):
            arrived(got.at[lax.rem(z + NZ - d, NZ)], base + d - 1, z=ring_z[0])
        carried, decays = jnp.zeros((DEPTH, STATES), F32), jnp.ones((1, STATES), F32)
        for k in order:
            state, decay = unpack(got, k)
            carried = decay * carried + state
            decays = decays * decay
        decays = jnp.broadcast_to(decays, (16, STATES))
        high = decays.astype(BF16)
        sent[:DEPTH, :] = carried.astype(BF16)
        sent[DEPTH : DEPTH + 16, :] = high
        sent[DEPTH + 16 :, :] = (decays - high.astype(F32)).astype(BF16)
        for d in range(1, NY):
            to = lax.rem(y + d, NY)
            send(sent, got_y.at[y], base + 7 + d - 1, y=to)
        got_y[pl.ds(y, 1)] = sent[...][None]

    def scan_back(got, got_y, sent, got_z, base, order, reverse):
        for d in range(1, NY):
            arrived(got_y.at[lax.rem(y + NY - d, NY)], base + 7 + d - 1, y=lax.rem(y + 1, NY))
        carried = jnp.zeros((DEPTH, STATES), F32)
        for k in reversed(range(NY)) if reverse else range(NY):
            state, decay = unpack(got_y, k)
            reached = (y < k) if reverse else (y > k)
            carried = jnp.where(reached, decay * carried + state, carried)
        for k in order:
            sent[k] = carried.astype(BF16)
            state, decay = unpack(got, k)
            carried = decay * carried + state
        for d in range(1, NZ):
            to = lax.rem(z + d, NZ)
            send(sent.at[to], got_z.at[z], base + 10 + d - 1, z=to)
        got_z[pl.ds(z, 1)] = sent[pl.ds(z, 1)]

    def scan_in(got_z, base, into):
        for d in range(1, NZ):
            arrived(got_z.at[lax.rem(z + NZ - d, NZ)], base + 10 + d - 1, z=ring_z[0])
        for k in range(HEADS):
            into[k * DEPTH : (k + 1) * DEPTH, :] = got_z[k]

    down, up = tuple(reversed(range(NZ))), tuple(range(NZ))

    scores = dot(b_ref[...], c_ref[...], ((1,), (1,)))
    low = lax.broadcasted_iota(jnp.int32, (RUN, 2 * DEPTH), 1) < DEPTH

    def within(pair):
        columns = slice(pair * 2 * DEPTH, (pair + 1) * 2 * DEPTH)
        part = dy_ref[:, columns]
        total = jnp.zeros((RUN, 2 * DEPTH), F32)
        for side in (0, 1):
            h = 2 * pair + side
            between = cum_t[h : h + 1, :] - cum[:, h : h + 1]
            decay = jnp.exp(jnp.where(two >= one, between, -1e30))
            dec[h] = decay
            kept = jnp.where(low if side == 0 else ~low, part, jnp.zeros_like(part))
            total = total + dot((decay * scores).astype(BF16), kept)
        gvi[:, columns] = total

    within(0)
    within(1)
    w_step(1)
    scan_rows(r1, b2, r2, M_BACK, down)
    x_relay()
    within(2)
    within(3)
    w_step(2)
    scan_back(r1, r2, b3, r3, M_BACK, down, True)
    w_step(3)
    scan_in(r3, M_BACK, gin)

    def g_part(ref, row):
        return rows(ref, row * RUN, RUN)

    grad_values = gvi[...] + dot(b_ref[...], gin[...], ((1,), (1,))) * shrink_x[...]
    gq[pl.ds(pl.multiple_of(y * RUN, RUN), RUN), :] = grad_values.astype(BF16)
    for d in (2, 1, 3):
        send(g_part(gq, y), g_part(gq, y), M_G + d - 1, y=lax.rem(y + d, NY))
    send(g_part(gq, y), g_part(gs, y), M_GS, core=other)

    w_step(4)
    theirs = pl.multiple_of(other * SLICE, SLICE)
    mine = pl.multiple_of(core * SLICE, SLICE)
    send(wq.at[pl.ds(theirs, SLICE), :], ws, M_WS, core=other)
    x_collect()
    own_x.wait()
    for d in (1, 3, 2):
        source = lax.rem(y + NY - d, NY)
        arrived(g_part(gq, source), M_G + d - 1, y=lax.rem(y + 1, NY))
        send(g_part(gq, source), g_part(gs, source), M_GS + d, core=other)
    for d in range(1, NY):
        arrived(x_part(lax.rem(y + NY - d, NY), other), M_XS + d - 1, core=other)

    def gw_own(dest):
        columns = pl.ds(pl.multiple_of(dest * RUN, RUN), RUN)
        return dot(xq[:, columns], gq[...], ((0,), (0,)))

    def gw_step(t):
        for way in (0, 1):
            dest = lax.rem(z + 4 - t, NZ) if way == 0 else lax.rem(z + 4 + t, NZ)
            own = gw_own(dest)
            for half in (way, 1 - way):
                if t == 0 and half != way:
                    continue
                part = own[half * HALF : (half + 1) * HALF]
                index = way * 8 + t * 2 + half
                if t > 1 or (t == 1 and half == way):
                    arrived(gwr.at[way, t - 1, half], M_GW + index - 2, z=ring_z[way])
                    part = part + gwr[way, t - 1, half].astype(F32)
                gws[way, t, half] = part.astype(BF16)
                send(gws.at[way, t, half], gwr.at[way, t, half], M_GW + index, z=ring_z[way])

    def gw_end():
        own = gw_own(z)
        for half in (0, 1):
            part = own[half * HALF : (half + 1) * HALF]
            for way in (0, 1):
                arrived(gwr.at[way, 3, half], M_GW + way * 8 + 6 + half, z=ring_z[way])
                part = part + gwr[way, 3, half].astype(F32)
            gw_ref[half * HALF : (half + 1) * HALF, :] = part

    def four_step(t, axis, me, own, sent, got, base):
        ends = []
        for way in (0, 1):
            dest = lax.rem(me + 3 - t, 4) if way == 0 else lax.rem(me + 1 + t, 4)
            to = lax.rem(me + 1, 4) if way == 0 else lax.rem(me + 3, 4)
            part = own(dest, way)
            if t > 0:
                arrived(got.at[way, t - 1], base + way * 3 + t - 1, **{axis: to})
                part = part + got[way, t - 1].astype(F32)
            if t < 3:
                sent[way, t] = part.astype(BF16)
                send(sent.at[way, t], got.at[way, t], base + way * 3 + t, **{axis: to})
            ends.append(part)
        return ends

    turn = lax.rem(x + NX - y, NX)

    def gi_rows(block, way, sub):
        return pl.ds(pl.multiple_of(block * RUN + way * HALF + sub * PIECE, PIECE), PIECE)

    def gi_product(d):
        block = pl.ds(pl.multiple_of(lax.rem(y + d, NY) * RUN, RUN), RUN)
        gia[block, :] = dot(gq[block, :], wq[pl.ds(mine, SLICE), :], ((1,), (1,))) + dot(
            gs[block, :], ws[...], ((1,), (1,))
        )

    def chain(slot):
        for way in (0, 1):
            place = lax.rem(turn + 3, NX) if way == 0 else lax.rem(7 - turn, NX)
            to = lax.rem(x + 1, NX) if way == 0 else lax.rem(x + 3, NX)
            i = slot - place

            @pl.when((i >= 0) & (i < 8))
            def _(way=way, place=place, to=to, i=i):
                block, sub = lax.rem(y + lax.div(i, 2), NY), lax.rem(i, 2)
                index = M_C + way * 8 + i
                own = gia[gi_rows(block, way, sub), :]

                @pl.when(place == 0)
                def _():
                    gis[way, pl.ds(i, 1)] = own.astype(BF16)[None]

                @pl.when(place > 0)
                def _():
                    arrived(gir.at[way, i], index, x=to)
                    gis[way, pl.ds(i, 1)] = (own[None] + gir[way, pl.ds(i, 1)].astype(F32)).astype(BF16)

                @pl.when(place < 3)
                def _():
                    message(gis.at[way, i], gir.at[way, i], index, x=to).start()

                @pl.when((place == 3) & (i < 2))
                def _():
                    gi_fin[gi_rows(0, way, sub), :] = gis[way, pl.ds(i, 1)][0]

                @pl.when((place == 3) & (i >= 2))
                def _():
                    message(
                        gis.at[way, i], gi_fin.at[gi_rows(0, way, sub), :], index, M_D + way * 2 + sub, y=block
                    ).start()

    gw_step(0)
    arrived(ws, M_WS, core=other)
    for d in range(NY):
        arrived(g_part(gs, lax.rem(y + NY - d, NY)), M_GS + d, core=other)
    gi_product(0)
    chain(0)
    gi_product(1)
    gi_product(2)
    gi_product(3)

    def product(k, _):
        block = pl.ds(pl.multiple_of(k * RUN, RUN), RUN)
        acc[block, :] = dot(xq[block, :], wq[...])
        return 0

    lax.fori_loop(0, NY, product, 0)

    def v_own(dest, half):
        return acc[pl.ds(pl.multiple_of(dest * RUN + half * HALF, HALF), HALF), :]

    def v_step(t):
        return four_step(t, "y", y, v_own, vs, vr, M_V)

    v_step(0)
    chain(1)
    gw_step(1)
    chain(2)
    v_step(1)
    chain(3)
    v_step(2)
    gw_step(2)
    chain(4)
    for half, part in enumerate(v_step(3)):
        vals[half * HALF : (half + 1) * HALF, :] = part.astype(BF16)
    xs[...] = (vals[...].astype(F32) * shrink_x[...]).astype(BF16)
    scan_pack(dot(xs[...], b_ref[...], ((0,), (0,))), f1)
    scan_out(f1, p1, M_FORE)
    chain(5)
    gw_step(3)
    chain(6)
    scan_rows(p1, f2, p2, M_FORE, up)

    mixed = jnp.zeros((RUN, RUN), F32)
    for pair in range(HEADS // 2):
        columns = slice(pair * 2 * DEPTH, (pair + 1) * 2 * DEPTH)
        part = vals[:, columns]
        for side in (0, 1):
            kept = jnp.where(low if side == 0 else ~low, part, jnp.zeros_like(part))
            mixed = mixed + dec[2 * pair + side] * dot(kept, dy_ref[:, columns], ((1,), (1,)))
    mixed = mixed.astype(BF16)
    grad_b = dot(mixed, c_ref[...]) + dot(xs[...], gin[...])
    grad_c = dot(mixed, b_ref[...], ((0,), (0,)))
    chain(7)
    scan_back(p1, p2, f3, p3, M_FORE, up, False)
    chain(8)
    gw_end()
    chain(9)
    scan_in(p3, M_FORE, hin)
    grad_c = grad_c + dot(dg[...], hin[...])

    sib_send[...] = jnp.where(core == 0, grad_c, grad_b)
    send(sib_send, sib_recv, M_S, core=other)
    arrived(sib_recv, M_S, core=other)
    red[pl.ds(x, 1)] = (jnp.where(core == 0, grad_b, grad_c) + sib_recv[...]).astype(BF16)[None]
    for d in range(1, NX):
        send(red.at[x], red.at[x], M_S + d, x=lax.rem(x + d, NX))
    chain(10)
    for d in range(1, NX):
        arrived(red.at[lax.rem(x + NX - d, NX)], M_S + d, x=lax.rem(x + 1, NX))
    total = red[0].astype(F32)
    for k in range(1, NX):
        total = total + red[k].astype(F32)
    tot_send[...] = total
    send(tot_send, tot_recv, M_S + 4, core=other)
    arrived(tot_recv, M_S + 4, core=other)
    gb_ref[...] = jnp.where(core == 0, tot_send[...], tot_recv[...])
    gc_ref[...] = jnp.where(core == 0, tot_recv[...], tot_send[...])

    @pl.when(x != y)
    def _():
        for way in (0, 1):
            for sub in (0, 1):
                arrived(gi_fin.at[gi_rows(0, way, sub), :], M_D + way * 2 + sub, y=x)

    gi_ref[...] = gi_fin[...]
    for way in (0, 1):
        for i in range(8):
            sent = message(gis.at[way, i], gir.at[way, i], M_C + way * 8 + i, x=lax.rem(x + 1, NX))
            if i >= 2:
                sent.wait_send()
            else:
                pl.when(x != y)(sent.wait_send)

    for copy in pending:
        copy.wait_send()


def hand_over(*refs):
    for source, result in zip(refs[:4], refs[4:], strict=True):
        result[...] = source[...]


def per_device(inputs, w_value, log_decay, b_proj, c_proj, grad_out):
    vmem = pl.BlockSpec(memory_space=pltpu.VMEM)

    def pair(count, *rest):
        return [pltpu.VMEM((count, *rest), BF16)] * 2

    scan = [
        *pair(HEADS, PACK, STATES),
        pltpu.VMEM((PACK, STATES), BF16),
        pltpu.VMEM((NY, PACK, STATES), BF16),
        *pair(HEADS, DEPTH, STATES),
    ]
    results = pl.pallas_call(
        kernel,
        out_shape=(
            jax.ShapeDtypeStruct((RUN, SLICE), BF16),
            jax.ShapeDtypeStruct((RUN, COLS), F32),
            jax.ShapeDtypeStruct((RUN, STATES), F32),
            jax.ShapeDtypeStruct((RUN, STATES), F32),
        ),
        in_specs=[pl.BlockSpec(memory_space=pl.ANY), vmem, vmem, vmem, vmem, vmem],
        out_specs=(vmem, vmem, vmem, vmem),
        scratch_shapes=[
            pltpu.VMEM((QUARTER, COLS), BF16),
            pltpu.VMEM((SLICE, COLS), BF16),
            pltpu.VMEM((NY * RUN, QUARTER), BF16),
            pltpu.VMEM((NY * RUN, COLS), BF16),
            pltpu.VMEM((NY * RUN, COLS), BF16),
            pltpu.VMEM((HEADS, RUN, RUN), F32),
            pltpu.VMEM((RUN, COLS), F32),
            pltpu.VMEM((RUN, COLS), F32),
            pltpu.VMEM((RUN, COLS), F32),
            pltpu.VMEM((RUN, COLS), BF16),
            pltpu.VMEM((RUN, COLS), BF16),
            pltpu.VMEM((RUN, COLS), BF16),
            pltpu.VMEM((HEADS * DEPTH, STATES), BF16),
            pltpu.VMEM((HEADS * DEPTH, STATES), BF16),
            *scan,
            *scan,
            pltpu.VMEM((NY * RUN, COLS), F32),
            pltpu.VMEM((NY * RUN, SLICE), F32),
            *pair(2, 3, HALF, COLS),
            *pair(2, 4, 2, HALF, COLS),
            *pair(2, 8, PIECE, SLICE),
            pltpu.VMEM((RUN, SLICE), BF16),
            pltpu.VMEM((RUN, STATES), F32),
            pltpu.VMEM((RUN, STATES), F32),
            pltpu.VMEM((NX, RUN, STATES), BF16),
            pltpu.VMEM((RUN, STATES), F32),
            pltpu.VMEM((RUN, STATES), F32),
            pltpu.SemaphoreType.DMA((MESSAGES,)),
            pltpu.SemaphoreType.DMA((MESSAGES,)),
            pltpu.SemaphoreType.DMA,
        ],
        compiler_params=pltpu.CompilerParams(
            collective_id=0, has_side_effects=True, vmem_limit_bytes=56 * 2**20
        ),
        name="ssd_backward",
    )(inputs, w_value, log_decay.T, b_proj, c_proj, grad_out)
    return pl.pallas_call(
        hand_over,
        out_shape=tuple(jax.ShapeDtypeStruct(r.shape, r.dtype) for r in results),
        in_specs=[vmem] * 4,
        out_specs=(vmem,) * 4,
        name="hand_over",
    )(*results)


def solution(mesh):
    grid = Mesh(mesh.devices.reshape(NY, NZ, NX, NC), ("y", "z", "x", "core"))
    seq, head = ("y", "z"), ("x", "core")
    placed = (P(seq, None), P(seq, head), P(seq, head), P(seq, None), P(seq, None), P(seq, head))
    return jax.shard_map(
        per_device,
        mesh=grid,
        in_specs=placed,
        out_specs=(P(seq, head), P(seq, head), P(seq, None), P(seq, None)),
        check_vma=False,
    )
```

```python
import jax
import jax.numpy as jnp
from jax import lax
from jax.experimental import pallas as pl
from jax.experimental.pallas import tpu as pltpu
from jax.sharding import Mesh
from jax.sharding import PartitionSpec as P

NY, NZ, NX, NC = 4, 8, 4, 2
RUN = 256
HALF = RUN // 2
COLS = 512
HEADS = 8
DEPTH = 64
STATES = 128
QUARTER = 2048
SLICE = 1024
SUB = 256
EIGHTH = RUN // 8
PIECE = 64
PACK = DEPTH + 16
F32, BF16 = jnp.float32, jnp.bfloat16
HIGH = lax.Precision.HIGHEST

M_W = 0
M_WS = M_W + 16
M_X = M_WS + 1
M_XX = M_X + 3
M_XS = M_XX + 9
M_BACK = M_XS + 3
M_FORE = M_BACK + 17
M_G = M_FORE + 17
M_GS = M_G + 3
M_V = M_GS + 4
M_GW = M_V + 3
M_C = M_GW + 16
M_D = M_C + 16
M_S = M_D + 4
MESSAGES = M_S + 14


def dot(a, b, dims=((1,), (0,)), precision=None):
    return lax.dot_general(a, b, (dims, ((), ())), preferred_element_type=F32, precision=precision)


def kernel(
    x_hbm, w_ref, log_t_ref, b_ref, c_ref, dy_ref,
    gi_ref, gw_ref, gb_ref, gc_ref,
    wq, ws, xq, gq, gs, dec, gvi, grow_x, shrink_x, dg, xs, vals, gin, hin,
    b1, r1, b2, r2, b3, r3, f1, p1, f2, p2, f3, p3,
    acc, gia, vs, vr, gws, gwr, gis, gir, gi_fin,
    part_send, part_recv, sums,
    send_sem, recv_sem, local_sem,
):
    y, z = lax.axis_index("y"), lax.axis_index("z")
    x, core = lax.axis_index("x"), lax.axis_index("core")
    other = 1 - core
    pending = []

    def message(src, dst, index, at=None, **to):
        return pltpu.make_async_remote_copy(
            src_ref=src, dst_ref=dst, send_sem=send_sem.at[index], recv_sem=recv_sem.at[index if at is None else at],
            device_id=to, device_id_type=pl.DeviceIdType.MESH,
        )

    def send(src, dst, index, **to):
        copy = message(src, dst, index, **to)
        copy.start()
        pending.append(copy)

    def arrived(dst, index, **to):
        message(dst, dst, index, **to).wait_recv()

    def rows(ref, start, size):
        return ref.at[pl.ds(pl.multiple_of(start, size), size), :]

    me = x * NC + core

    def group_peer(e):
        to = lax.rem(me + e, NX * NC)
        return {"x": lax.div(to, NC), "core": lax.rem(to, NC)}

    barrier = pltpu.get_barrier_semaphore()
    for d in range(1, NZ):
        pl.semaphore_signal(barrier, inc=1, device_id={"z": lax.rem(z + d, NZ)}, device_id_type=pl.DeviceIdType.MESH)
    for d in range(1, NY):
        pl.semaphore_signal(barrier, inc=1, device_id={"y": lax.rem(y + d, NY)}, device_id_type=pl.DeviceIdType.MESH)
    for e in range(1, NX * NC):
        pl.semaphore_signal(barrier, inc=1, device_id=group_peer(e), device_id_type=pl.DeviceIdType.MESH)
    own_x = pltpu.make_async_copy(
        x_hbm.at[:, pl.ds(pl.multiple_of(y * QUARTER, QUARTER), QUARTER)], rows(xq, y * RUN, RUN), local_sem
    )
    own_x.start()
    wq[pl.ds(pl.multiple_of(z * RUN, RUN), RUN), :] = w_ref[...]

    one = lax.broadcasted_iota(jnp.int32, (RUN, RUN), 0)
    two = lax.broadcasted_iota(jnp.int32, (RUN, RUN), 1)
    logs = log_t_ref[...]
    cum = dot((one >= two).astype(F32), logs, ((1,), (1,)), HIGH)
    cum_t = dot(logs, (one <= two).astype(F32), precision=HIGH)
    head_of = lax.broadcasted_iota(jnp.int32, (HEADS, COLS), 1) // DEPTH
    spread = (lax.broadcasted_iota(jnp.int32, (HEADS, COLS), 0) == head_of).astype(F32)
    cum_x = dot(cum, spread, precision=HIGH)
    grow_x[...] = jnp.exp(cum_x)
    shrink_x[...] = jnp.exp(cum_x[RUN - 1 :, :] - cum_x)
    dg[...] = (dy_ref[...].astype(F32) * grow_x[...]).astype(BF16)

    first_rows = lax.broadcasted_iota(jnp.int32, (16, STATES), 0) < 8

    def two_terms(decay):
        decay = jnp.broadcast_to(decay, (16, STATES))
        high = decay.astype(BF16).astype(F32)
        return jnp.where(first_rows, high, decay - high).astype(BF16)

    def scan_pack(states, sent):
        for k in range(HEADS):
            sent[k, :DEPTH, :] = states[k * DEPTH : (k + 1) * DEPTH].astype(BF16)

    def scan_out(sent, got, base):
        for d in (4, 3, 5, 2, 6, 1, 7):
            to = lax.rem(z + d, NZ)
            send(sent.at[to], got.at[z], base + d - 1, z=to)
        got[pl.ds(z, 1)] = sent[pl.ds(z, 1)]

    scan_pack(dot(dg[...], c_ref[...], ((0,), (0,))), b1)
    for k in range(HEADS):
        b1[k, DEPTH:, :] = two_terms(jnp.exp(cum[RUN - 1 :, k : k + 1]))
    pl.semaphore_wait(barrier, NZ + NY + NX * NC - 3)
    scan_out(b1, r1, M_BACK)

    ring_z = (lax.rem(z + 1, NZ), lax.rem(z + NZ - 1, NZ))

    def w_part(shard, half):
        return rows(wq, shard * RUN + half * HALF, HALF)

    def w_send(way, hop, half):
        shard = lax.rem(z + NZ - (hop - 1), NZ) if way == 0 else lax.rem(z + (hop - 1), NZ)
        send(w_part(shard, half), w_part(shard, half), M_W + way * 8 + (hop - 1) * 2 + half, z=ring_z[way])

    def w_step(hop):
        for half in (0, 1):
            for way in (0, 1):
                if hop == NZ // 2 and half != way:
                    continue
                shard = lax.rem(z + NZ - hop, NZ) if way == 0 else lax.rem(z + hop, NZ)
                arrived(w_part(shard, half), M_W + way * 8 + (hop - 1) * 2 + half, z=ring_z[way])
                if hop < NZ // 2 - 1 or (hop == NZ // 2 - 1 and half == way):
                    w_send(way, hop + 1, half)

    for half in (0, 1):
        for way in (0, 1):
            w_send(way, 1, half)

    def x_part(row, col):
        return xq.at[
            pl.ds(pl.multiple_of(row * RUN, RUN), RUN), pl.ds(pl.multiple_of(col * SLICE, SLICE), SLICE)
        ]

    def x_piece(row, sub):
        return xq.at[
            pl.ds(pl.multiple_of(row * RUN, RUN), RUN), pl.ds(pl.multiple_of(core * SLICE + sub * SUB, SUB), SUB)
        ]

    for d in (2, 1, 3):
        to = lax.rem(y + d, NY)
        columns = pl.ds(pl.multiple_of(to * QUARTER + core * SLICE + x * SUB, SUB), SUB)
        send(x_hbm.at[:, columns], x_piece(y, x), M_X + d - 1, y=to)

    def x_relay():
        for d in (1, 3, 2):
            source = lax.rem(y + NY - d, NY)
            arrived(x_piece(source, x), M_X + d - 1, y=lax.rem(y + 1, NY))
            for e in (2, 1, 3):
                send(x_piece(source, x), x_piece(source, x), M_XX + (d - 1) * 3 + e - 1, x=lax.rem(x + e, NX))

    def x_collect():
        for d in (1, 3, 2):
            source = lax.rem(y + NY - d, NY)
            for e in (1, 2, 3):
                arrived(x_piece(source, lax.rem(x + NX - e, NX)), M_XX + (d - 1) * 3 + e - 1, x=lax.rem(x + 1, NX))
            send(x_part(source, core), x_part(source, core), M_XS + d - 1, core=other)

    def unpack(ref, decays, k):
        terms = decays[k, DEPTH:, :].astype(F32)
        return ref[k, :DEPTH, :].astype(F32), terms[:1, :] + terms[8:9, :]

    def scan_rows(got, sent, got_y, base, order, with_decay):
        for d in range(1, NZ):
            arrived(got.at[lax.rem(z + NZ - d, NZ)], base + d - 1, z=ring_z[0])
        carried, decays = jnp.zeros((DEPTH, STATES), F32), jnp.ones((1, STATES), F32)
        for k in order:
            state, decay = unpack(got, r1, k)
            carried = decay * carried + state
            decays = decays * decay
        sent[:DEPTH, :] = carried.astype(BF16)
        if with_decay:
            sent[DEPTH:, :] = two_terms(decays)
        for d in (2, 1, 3):
            to = lax.rem(y + d, NY)
            send(sent, got_y.at[y], base + 7 + d - 1, y=to)
        got_y[pl.ds(y, 1)] = sent[...][None]

    def scan_back(got, got_y, sent, got_z, base, order, reverse):
        for d in range(1, NY):
            arrived(got_y.at[lax.rem(y + NY - d, NY)], base + 7 + d - 1, y=lax.rem(y + 1, NY))
        carried = jnp.zeros((DEPTH, STATES), F32)
        for k in reversed(range(NY)) if reverse else range(NY):
            state, decay = unpack(got_y, r2, k)
            reached = (y < k) if reverse else (y > k)
            carried = jnp.where(reached, decay * carried + state, carried)
        for k in order:
            sent[k] = carried.astype(BF16)
            state, decay = unpack(got, r1, k)
            carried = decay * carried + state
        for d in (4, 3, 5, 2, 6, 1, 7):
            to = lax.rem(z + d, NZ)
            send(sent.at[to], got_z.at[z], base + 10 + d - 1, z=to)
        got_z[pl.ds(z, 1)] = sent[pl.ds(z, 1)]

    def scan_in(got_z, base, into):
        for d in range(1, NZ):
            arrived(got_z.at[lax.rem(z + NZ - d, NZ)], base + 10 + d - 1, z=ring_z[0])
        for k in range(HEADS):
            into[k * DEPTH : (k + 1) * DEPTH, :] = got_z[k]

    down, up = tuple(reversed(range(NZ))), tuple(range(NZ))

    scores = dot(b_ref[...], c_ref[...], ((1,), (1,)))
    low = lax.broadcasted_iota(jnp.int32, (RUN, 2 * DEPTH), 1) < DEPTH

    def within(pair):
        columns = slice(pair * 2 * DEPTH, (pair + 1) * 2 * DEPTH)
        part = dy_ref[:, columns]
        total = jnp.zeros((RUN, 2 * DEPTH), F32)
        for side in (0, 1):
            h = 2 * pair + side
            between = cum_t[h : h + 1, :] - cum[:, h : h + 1]
            decay = jnp.exp(jnp.where(two >= one, between, -1e30))
            dec[h] = decay
            kept = jnp.where(low if side == 0 else ~low, part, jnp.zeros_like(part))
            total = total + dot((decay * scores).astype(BF16), kept)
        gvi[:, columns] = total

    for pair in range(HEADS // 2):
        within(pair)
    scan_rows(r1, b2, r2, M_BACK, down, True)
    scan_back(r1, r2, b3, r3, M_BACK, down, True)
    x_relay()
    w_step(1)
    scan_in(r3, M_BACK, gin)

    def g_part(ref, row):
        return rows(ref, row * RUN, RUN)

    grad_values = gvi[...] + dot(b_ref[...], gin[...], ((1,), (1,))) * shrink_x[...]
    gq[pl.ds(pl.multiple_of(y * RUN, RUN), RUN), :] = grad_values.astype(BF16)
    for d in (2, 1, 3):
        send(g_part(gq, y), g_part(gq, y), M_G + d - 1, y=lax.rem(y + d, NY))
    send(g_part(gq, y), g_part(gs, y), M_GS, core=other)

    w_step(2)
    w_step(3)
    for d in (1, 3, 2):
        source = lax.rem(y + NY - d, NY)
        arrived(g_part(gq, source), M_G + d - 1, y=lax.rem(y + 1, NY))
        send(g_part(gq, source), g_part(gs, source), M_GS + d, core=other)
    w_step(4)
    theirs = pl.multiple_of(other * SLICE, SLICE)
    mine = pl.multiple_of(core * SLICE, SLICE)
    send(wq.at[pl.ds(theirs, SLICE), :], ws, M_WS, core=other)
    x_collect()
    own_x.wait()

    def gw_own(dest):
        columns = pl.ds(pl.multiple_of(dest * RUN, RUN), RUN)
        return dot(xq[:, columns], gq[...], ((0,), (0,)))

    def gw_step(t):
        dests = (lax.rem(z + 4 - t, NZ), lax.rem(z + 4 + t, NZ))
        own = [gw_own(dest) for dest in dests]
        for way, half in ((0, 0), (1, 1), (0, 1), (1, 0)):
            if t == 0 and half != way:
                continue
            part = own[way][half * HALF : (half + 1) * HALF]
            index = way * 8 + t * 2 + half
            if t > 1 or (t == 1 and half == way):
                arrived(gwr.at[way, t - 1, half], M_GW + index - 2, z=ring_z[way])
                part = part + gwr[way, t - 1, half].astype(F32)
            gws[way, t, half] = part.astype(BF16)
            send(gws.at[way, t, half], gwr.at[way, t, half], M_GW + index, z=ring_z[way])

    def gw_end():
        own = gw_own(z)
        for half in (0, 1):
            part = own[half * HALF : (half + 1) * HALF]
            for way in (0, 1):
                arrived(gwr.at[way, 3, half], M_GW + way * 8 + 6 + half, z=ring_z[way])
                part = part + gwr[way, 3, half].astype(F32)
            gw_ref[half * HALF : (half + 1) * HALF, :] = part

    turn = lax.rem(x + NX - y, NX)

    def gi_rows(block, way, sub):
        return pl.ds(pl.multiple_of(block * RUN + way * HALF + sub * PIECE, PIECE), PIECE)

    def gi_product(d):
        block = pl.ds(pl.multiple_of(lax.rem(y + d, NY) * RUN, RUN), RUN)
        gia[block, :] = dot(gq[block, :], wq[pl.ds(mine, SLICE), :], ((1,), (1,))) + dot(
            gs[block, :], ws[...], ((1,), (1,))
        )

    def chain(slot):
        chain_step(slot, False)

    def chain_start():
        for i in range(8):
            chain_step(i, True)

    def chain_step(slot, start):
        for way in (0, 1):
            place = lax.rem(turn + 3, NX) if way == 0 else lax.rem(7 - turn, NX)
            to = lax.rem(x + 1, NX) if way == 0 else lax.rem(x + 3, NX)
            i = slot if start else slot - place

            @pl.when((place == 0) if start else ((place > 0) & (i >= 0) & (i < 8)))
            def _(way=way, place=place, to=to, i=i):
                block, sub = lax.rem(y + 1 + lax.div(i, 2), NY), lax.rem(i, 2)
                index = M_C + way * 8 + i
                own = gia[gi_rows(block, way, sub), :]

                if start:
                    gis[way, i] = own.astype(BF16)
                    message(gis.at[way, i], gir.at[way, i], index, x=to).start()
                    return
                arrived(gir.at[way, i], index, x=to)
                gis[way, pl.ds(i, 1)] = (own[None] + gir[way, pl.ds(i, 1)].astype(F32)).astype(BF16)

                @pl.when(place < 3)
                def _():
                    message(gis.at[way, i], gir.at[way, i], index, x=to).start()

                @pl.when((place == 3) & (i >= 6))
                def _():
                    gi_fin[gi_rows(0, way, sub), :] = gis[way, pl.ds(i, 1)][0]

                @pl.when((place == 3) & (i < 6))
                def _():
                    message(
                        gis.at[way, i], gi_fin.at[gi_rows(0, way, sub), :], index, M_D + way * 2 + sub, y=block
                    ).start()

    def product(start):
        def one_run(k, _):
            block = pl.ds(pl.multiple_of(k * RUN, RUN), RUN)
            part = dot(xq[block, pl.ds(start, SLICE)], wq[pl.ds(start, SLICE), :])
            acc[block, :] = part if start is mine else acc[block, :] + part
            return 0

        lax.fori_loop(0, NY, one_run, 0)

    def v_send():
        for d in (2, 1, 3):
            to = lax.rem(y + d, NY)
            vs[d - 1] = acc[pl.ds(pl.multiple_of(to * RUN, RUN), RUN), :].astype(BF16)
            send(vs.at[d - 1], vr.at[d - 1], M_V + d - 1, y=to)

    def v_end():
        total = acc[pl.ds(pl.multiple_of(y * RUN, RUN), RUN), :]
        for d in (1, 3, 2):
            arrived(vr.at[d - 1], M_V + d - 1, y=lax.rem(y + 1, NY))
            total = total + vr[d - 1].astype(F32)
        vals[...] = total.astype(BF16)
        xs[...] = (vals[...].astype(F32) * shrink_x[...]).astype(BF16)

    product(mine)
    arrived(ws, M_WS, core=other)
    for d in range(NY):
        arrived(g_part(gs, lax.rem(y + NY - d, NY)), M_GS + d, core=other)
    for d in range(NY):
        gi_product(d)
    chain_start()
    for d in range(1, NY):
        arrived(x_part(lax.rem(y + NY - d, NY), other), M_XS + d - 1, core=other)
    product(theirs)
    v_send()
    gw_step(0)
    chain(1)
    chain(2)
    gw_step(1)
    chain(3)
    v_end()
    scan_pack(dot(xs[...], b_ref[...], ((0,), (0,))), f1)
    scan_out(f1, p1, M_FORE)
    chain(4)
    gw_step(2)
    scan_rows(p1, f2, p2, M_FORE, up, False)
    chain(5)
    gw_step(3)
    chain(6)

    mixed = jnp.zeros((RUN, RUN), F32)
    for pair in range(HEADS // 2):
        columns = slice(pair * 2 * DEPTH, (pair + 1) * 2 * DEPTH)
        part = vals[:, columns]
        for side in (0, 1):
            kept = jnp.where(low if side == 0 else ~low, part, jnp.zeros_like(part))
            mixed = mixed + dec[2 * pair + side] * dot(kept, dy_ref[:, columns], ((1,), (1,)))
    mixed = mixed.astype(BF16)
    grad_b = dot(mixed, c_ref[...]) + dot(xs[...], gin[...])
    grad_c = dot(mixed, b_ref[...], ((0,), (0,)))
    scan_back(p1, p2, f3, p3, M_FORE, up, False)
    chain(7)
    gw_end()
    chain(8)
    scan_in(p3, M_FORE, hin)
    grad_c = grad_c + dot(dg[...], hin[...])

    for k in range(NX * NC):
        share = slice(k * EIGHTH, (k + 1) * EIGHTH)
        part_send[k, :EIGHTH, :] = grad_b[share].astype(BF16)
        part_send[k, EIGHTH:, :] = grad_c[share].astype(BF16)
    for e in range(1, NX * NC):
        send(part_send.at[lax.rem(me + e, NX * NC)], part_recv.at[me], M_S + e - 1, **group_peer(e))
    part_recv[pl.ds(me, 1)] = part_send[pl.ds(me, 1)]
    chain(9)
    for e in range(1, NX * NC):
        arrived(part_recv.at[lax.rem(me + NX * NC - e, NX * NC)], M_S + e - 1, **group_peer(e))
    total = part_recv[0].astype(F32)
    for k in range(1, NX * NC):
        total = total + part_recv[k].astype(F32)
    sums[pl.ds(me, 1)] = total.astype(BF16)[None]
    for e in range(1, NX * NC):
        send(sums.at[me], sums.at[me], M_S + 7 + e - 1, **group_peer(e))
    chain(10)
    for e in range(1, NX * NC):
        arrived(sums.at[lax.rem(me + NX * NC - e, NX * NC)], M_S + 7 + e - 1, **group_peer(e))
    for k in range(NX * NC):
        share = slice(k * EIGHTH, (k + 1) * EIGHTH)
        gb_ref[share, :] = sums[k, :EIGHTH, :].astype(F32)
        gc_ref[share, :] = sums[k, EIGHTH:, :].astype(F32)

    @pl.when(x != y)
    def _():
        for way in (0, 1):
            for sub in (0, 1):
                arrived(gi_fin.at[gi_rows(0, way, sub), :], M_D + way * 2 + sub, y=x)

    gi_ref[...] = gi_fin[...]
    for way in (0, 1):
        for i in range(8):
            sent = message(gis.at[way, i], gir.at[way, i], M_C + way * 8 + i, x=lax.rem(x + 1, NX))
            if i < 6:
                sent.wait_send()
            else:
                pl.when(x != y)(sent.wait_send)

    for copy in pending:
        copy.wait_send()


def hand_over(*refs):
    for source, result in zip(refs[:4], refs[4:], strict=True):
        result[...] = source[...]


def per_device(inputs, w_value, log_decay, b_proj, c_proj, grad_out):
    vmem = pl.BlockSpec(memory_space=pltpu.VMEM)

    def pair(count, *rest):
        return [pltpu.VMEM((count, *rest), BF16)] * 2

    def scan(rows):
        return [
            *pair(HEADS, rows, STATES),
            pltpu.VMEM((rows, STATES), BF16),
            pltpu.VMEM((NY, rows, STATES), BF16),
            *pair(HEADS, DEPTH, STATES),
        ]

    results = pl.pallas_call(
        kernel,
        out_shape=(
            jax.ShapeDtypeStruct((RUN, SLICE), BF16),
            jax.ShapeDtypeStruct((RUN, COLS), F32),
            jax.ShapeDtypeStruct((RUN, STATES), F32),
            jax.ShapeDtypeStruct((RUN, STATES), F32),
        ),
        in_specs=[pl.BlockSpec(memory_space=pl.ANY), vmem, vmem, vmem, vmem, vmem],
        out_specs=(vmem, vmem, vmem, vmem),
        scratch_shapes=[
            pltpu.VMEM((QUARTER, COLS), BF16),
            pltpu.VMEM((SLICE, COLS), BF16),
            pltpu.VMEM((NY * RUN, QUARTER), BF16),
            pltpu.VMEM((NY * RUN, COLS), BF16),
            pltpu.VMEM((NY * RUN, COLS), BF16),
            pltpu.VMEM((HEADS, RUN, RUN), F32),
            pltpu.VMEM((RUN, COLS), F32),
            pltpu.VMEM((RUN, COLS), F32),
            pltpu.VMEM((RUN, COLS), F32),
            pltpu.VMEM((RUN, COLS), BF16),
            pltpu.VMEM((RUN, COLS), BF16),
            pltpu.VMEM((RUN, COLS), BF16),
            pltpu.VMEM((HEADS * DEPTH, STATES), BF16),
            pltpu.VMEM((HEADS * DEPTH, STATES), BF16),
            *scan(PACK),
            *scan(DEPTH),
            pltpu.VMEM((NY * RUN, COLS), F32),
            pltpu.VMEM((NY * RUN, SLICE), F32),
            *pair(3, RUN, COLS),
            *pair(2, 4, 2, HALF, COLS),
            *pair(2, 8, PIECE, SLICE),
            pltpu.VMEM((RUN, SLICE), BF16),
            *pair(NX * NC, 2 * EIGHTH, STATES),
            pltpu.VMEM((NX * NC, 2 * EIGHTH, STATES), BF16),
            pltpu.SemaphoreType.DMA((MESSAGES,)),
            pltpu.SemaphoreType.DMA((MESSAGES,)),
            pltpu.SemaphoreType.DMA,
        ],
        compiler_params=pltpu.CompilerParams(
            collective_id=0, has_side_effects=True, vmem_limit_bytes=56 * 2**20
        ),
        name="ssd_backward",
    )(inputs, w_value, log_decay.T, b_proj, c_proj, grad_out)
    return pl.pallas_call(
        hand_over,
        out_shape=tuple(jax.ShapeDtypeStruct(r.shape, r.dtype) for r in results),
        in_specs=[vmem] * 4,
        out_specs=(vmem,) * 4,
        name="hand_over",
    )(*results)


def solution(mesh):
    grid = Mesh(mesh.devices.reshape(NY, NZ, NX, NC), ("y", "z", "x", "core"))
    seq, head = ("y", "z"), ("x", "core")
    placed = (P(seq, None), P(seq, head), P(seq, head), P(seq, None), P(seq, None), P(seq, head))
    return jax.shard_map(
        per_device,
        mesh=grid,
        in_specs=placed,
        out_specs=(P(seq, head), P(seq, head), P(seq, None), P(seq, None)),
        check_vma=False,
    )
```

```python
import jax
import jax.numpy as jnp
from jax import lax
from jax.experimental import pallas as pl
from jax.experimental.pallas import tpu as pltpu
from jax.sharding import Mesh
from jax.sharding import PartitionSpec as P

NY, NZ, NX, NC = 4, 8, 4, 2
RUN = 256
HALF = RUN // 2
COLS = 512
HEADS = 8
DEPTH = 64
STATES = 128
QUARTER = 2048
SLICE = 1024
SUB = 256
EIGHTH = RUN // 8
PIECE = 64
PACK = DEPTH + 16
F32, BF16 = jnp.float32, jnp.bfloat16
HIGH = lax.Precision.HIGHEST

M_W = 0
M_WS = M_W + 16
M_X = M_WS + 1
M_XX = M_X + 3
M_XS = M_XX + 9
M_BACK = M_XS + 3
M_FORE = M_BACK + 17
M_G = M_FORE + 17
M_GS = M_G + 3
M_V = M_GS + 4
M_GW = M_V + 6
M_C = M_GW + 16
M_D = M_C + 16
M_S = M_D + 4
MESSAGES = M_S + 14


def dot(a, b, dims=((1,), (0,)), precision=None):
    return lax.dot_general(a, b, (dims, ((), ())), preferred_element_type=F32, precision=precision)


def kernel(
    x_hbm, w_ref, log_t_ref, b_ref, c_ref, dy_ref,
    gi_ref, gw_ref, gb_ref, gc_ref,
    wq, ws, xq, gq, gs, dec, gvi, grow_x, shrink_x, dg, xs, vals, gin, hin,
    b1, r1, b2, r2, b3, r3, f1, p1, f2, p2, f3, p3,
    acc, gia, vs, vr, gws, gwr, gis, gir, gi_fin,
    part_send, part_recv, sums,
    send_sem, recv_sem, local_sem,
):
    y, z = lax.axis_index("y"), lax.axis_index("z")
    x, core = lax.axis_index("x"), lax.axis_index("core")
    other = 1 - core
    pending = []

    def message(src, dst, index, at=None, **to):
        return pltpu.make_async_remote_copy(
            src_ref=src, dst_ref=dst, send_sem=send_sem.at[index], recv_sem=recv_sem.at[index if at is None else at],
            device_id=to, device_id_type=pl.DeviceIdType.MESH,
        )

    def send(src, dst, index, **to):
        copy = message(src, dst, index, **to)
        copy.start()
        pending.append(copy)

    def arrived(dst, index, **to):
        message(dst, dst, index, **to).wait_recv()

    def rows(ref, start, size):
        return ref.at[pl.ds(pl.multiple_of(start, size), size), :]

    me = x * NC + core

    def group_peer(e):
        to = lax.rem(me + e, NX * NC)
        return {"x": lax.div(to, NC), "core": lax.rem(to, NC)}

    barrier = pltpu.get_barrier_semaphore()
    for d in range(1, NZ):
        pl.semaphore_signal(barrier, inc=1, device_id={"z": lax.rem(z + d, NZ)}, device_id_type=pl.DeviceIdType.MESH)
    for d in range(1, NY):
        pl.semaphore_signal(barrier, inc=1, device_id={"y": lax.rem(y + d, NY)}, device_id_type=pl.DeviceIdType.MESH)
    for e in range(1, NX * NC):
        pl.semaphore_signal(barrier, inc=1, device_id=group_peer(e), device_id_type=pl.DeviceIdType.MESH)
    own_x = pltpu.make_async_copy(
        x_hbm.at[:, pl.ds(pl.multiple_of(y * QUARTER, QUARTER), QUARTER)], rows(xq, y * RUN, RUN), local_sem
    )
    own_x.start()
    wq[pl.ds(pl.multiple_of(z * RUN, RUN), RUN), :] = w_ref[...]

    one = lax.broadcasted_iota(jnp.int32, (RUN, RUN), 0)
    two = lax.broadcasted_iota(jnp.int32, (RUN, RUN), 1)
    logs = log_t_ref[...]
    cum = dot((one >= two).astype(F32), logs, ((1,), (1,)), HIGH)
    cum_t = dot(logs, (one <= two).astype(F32), precision=HIGH)
    head_of = lax.broadcasted_iota(jnp.int32, (HEADS, COLS), 1) // DEPTH
    spread = (lax.broadcasted_iota(jnp.int32, (HEADS, COLS), 0) == head_of).astype(F32)
    cum_x = dot(cum, spread, precision=HIGH)
    grow_x[...] = jnp.exp(cum_x)
    shrink_x[...] = jnp.exp(cum_x[RUN - 1 :, :] - cum_x)
    dg[...] = (dy_ref[...].astype(F32) * grow_x[...]).astype(BF16)

    first_rows = lax.broadcasted_iota(jnp.int32, (16, STATES), 0) < 8

    def two_terms(decay):
        decay = jnp.broadcast_to(decay, (16, STATES))
        high = decay.astype(BF16).astype(F32)
        return jnp.where(first_rows, high, decay - high).astype(BF16)

    def scan_pack(states, sent):
        for k in range(HEADS):
            sent[k, :DEPTH, :] = states[k * DEPTH : (k + 1) * DEPTH].astype(BF16)

    def scan_out(sent, got, base):
        for d in (4, 3, 5, 2, 6, 1, 7):
            to = lax.rem(z + d, NZ)
            send(sent.at[to], got.at[z], base + d - 1, z=to)
        got[pl.ds(z, 1)] = sent[pl.ds(z, 1)]

    scan_pack(dot(dg[...], c_ref[...], ((0,), (0,))), b1)
    for k in range(HEADS):
        b1[k, DEPTH:, :] = two_terms(jnp.exp(cum[RUN - 1 :, k : k + 1]))
    pl.semaphore_wait(barrier, NZ + NY + NX * NC - 3)
    scan_out(b1, r1, M_BACK)

    ring_z = (lax.rem(z + 1, NZ), lax.rem(z + NZ - 1, NZ))

    def w_part(shard, half):
        return rows(wq, shard * RUN + half * HALF, HALF)

    def w_send(way, hop, half):
        shard = lax.rem(z + NZ - (hop - 1), NZ) if way == 0 else lax.rem(z + (hop - 1), NZ)
        send(w_part(shard, half), w_part(shard, half), M_W + way * 8 + (hop - 1) * 2 + half, z=ring_z[way])

    def w_step(hop):
        for half in (0, 1):
            for way in (0, 1):
                if hop == NZ // 2 and half != way:
                    continue
                shard = lax.rem(z + NZ - hop, NZ) if way == 0 else lax.rem(z + hop, NZ)
                arrived(w_part(shard, half), M_W + way * 8 + (hop - 1) * 2 + half, z=ring_z[way])
                if hop < NZ // 2 - 1 or (hop == NZ // 2 - 1 and half == way):
                    w_send(way, hop + 1, half)

    for half in (0, 1):
        for way in (0, 1):
            w_send(way, 1, half)

    def x_part(row, col):
        return xq.at[
            pl.ds(pl.multiple_of(row * RUN, RUN), RUN), pl.ds(pl.multiple_of(col * SLICE, SLICE), SLICE)
        ]

    def x_piece(row, sub):
        return xq.at[
            pl.ds(pl.multiple_of(row * RUN, RUN), RUN), pl.ds(pl.multiple_of(core * SLICE + sub * SUB, SUB), SUB)
        ]

    for d in (2, 1, 3):
        to = lax.rem(y + d, NY)
        columns = pl.ds(pl.multiple_of(to * QUARTER + core * SLICE + x * SUB, SUB), SUB)
        send(x_hbm.at[:, columns], x_piece(y, x), M_X + d - 1, y=to)

    def x_relay():
        for d in (1, 3, 2):
            source = lax.rem(y + NY - d, NY)
            arrived(x_piece(source, x), M_X + d - 1, y=lax.rem(y + 1, NY))
            for e in (2, 1, 3):
                send(x_piece(source, x), x_piece(source, x), M_XX + (d - 1) * 3 + e - 1, x=lax.rem(x + e, NX))

    def x_collect():
        for d in (1, 3, 2):
            source = lax.rem(y + NY - d, NY)
            for e in (1, 2, 3):
                arrived(x_piece(source, lax.rem(x + NX - e, NX)), M_XX + (d - 1) * 3 + e - 1, x=lax.rem(x + 1, NX))
            send(x_part(source, core), x_part(source, core), M_XS + d - 1, core=other)

    def unpack(ref, decays, k):
        terms = decays[k, DEPTH:, :].astype(F32)
        return ref[k, :DEPTH, :].astype(F32), terms[:1, :] + terms[8:9, :]

    def scan_rows(got, sent, got_y, base, order, with_decay):
        for d in range(1, NZ):
            arrived(got.at[lax.rem(z + NZ - d, NZ)], base + d - 1, z=ring_z[0])
        carried, decays = jnp.zeros((DEPTH, STATES), F32), jnp.ones((1, STATES), F32)
        for k in order:
            state, decay = unpack(got, r1, k)
            carried = decay * carried + state
            decays = decays * decay
        sent[:DEPTH, :] = carried.astype(BF16)
        if with_decay:
            sent[DEPTH:, :] = two_terms(decays)
        for d in (2, 1, 3):
            to = lax.rem(y + d, NY)
            send(sent, got_y.at[y], base + 7 + d - 1, y=to)
        got_y[pl.ds(y, 1)] = sent[...][None]

    def scan_back(got, got_y, sent, got_z, base, order, reverse):
        for d in range(1, NY):
            arrived(got_y.at[lax.rem(y + NY - d, NY)], base + 7 + d - 1, y=lax.rem(y + 1, NY))
        carried = jnp.zeros((DEPTH, STATES), F32)
        for k in reversed(range(NY)) if reverse else range(NY):
            state, decay = unpack(got_y, r2, k)
            reached = (y < k) if reverse else (y > k)
            carried = jnp.where(reached, decay * carried + state, carried)
        for k in order:
            sent[k] = carried.astype(BF16)
            state, decay = unpack(got, r1, k)
            carried = decay * carried + state
        for d in (4, 3, 5, 2, 6, 1, 7):
            to = lax.rem(z + d, NZ)
            send(sent.at[to], got_z.at[z], base + 10 + d - 1, z=to)
        got_z[pl.ds(z, 1)] = sent[pl.ds(z, 1)]

    def scan_in(got_z, base, into):
        for d in range(1, NZ):
            arrived(got_z.at[lax.rem(z + NZ - d, NZ)], base + 10 + d - 1, z=ring_z[0])
        for k in range(HEADS):
            into[k * DEPTH : (k + 1) * DEPTH, :] = got_z[k]

    down, up = tuple(reversed(range(NZ))), tuple(range(NZ))

    scores = dot(b_ref[...], c_ref[...], ((1,), (1,)))
    low = lax.broadcasted_iota(jnp.int32, (RUN, 2 * DEPTH), 1) < DEPTH

    def within(pair):
        columns = slice(pair * 2 * DEPTH, (pair + 1) * 2 * DEPTH)
        part = dy_ref[:, columns]
        total = jnp.zeros((RUN, 2 * DEPTH), F32)
        for side in (0, 1):
            h = 2 * pair + side
            between = cum_t[h : h + 1, :] - cum[:, h : h + 1]
            decay = jnp.exp(jnp.where(two >= one, between, -1e30))
            dec[h] = decay
            kept = jnp.where(low if side == 0 else ~low, part, jnp.zeros_like(part))
            total = total + dot((decay * scores).astype(BF16), kept)
        gvi[:, columns] = total

    for pair in range(HEADS // 2):
        within(pair)
    scan_rows(r1, b2, r2, M_BACK, down, True)
    scan_back(r1, r2, b3, r3, M_BACK, down, True)
    x_relay()
    w_step(1)
    scan_in(r3, M_BACK, gin)

    def g_part(ref, row):
        return rows(ref, row * RUN, RUN)

    grad_values = gvi[...] + dot(b_ref[...], gin[...], ((1,), (1,))) * shrink_x[...]
    gq[pl.ds(pl.multiple_of(y * RUN, RUN), RUN), :] = grad_values.astype(BF16)
    for d in (2, 1, 3):
        send(g_part(gq, y), g_part(gq, y), M_G + d - 1, y=lax.rem(y + d, NY))
    send(g_part(gq, y), g_part(gs, y), M_GS, core=other)

    w_step(2)
    w_step(3)
    for d in (1, 3, 2):
        source = lax.rem(y + NY - d, NY)
        arrived(g_part(gq, source), M_G + d - 1, y=lax.rem(y + 1, NY))
        send(g_part(gq, source), g_part(gs, source), M_GS + d, core=other)
    w_step(4)
    theirs = pl.multiple_of(other * SLICE, SLICE)
    mine = pl.multiple_of(core * SLICE, SLICE)
    send(wq.at[pl.ds(theirs, SLICE), :], ws, M_WS, core=other)
    x_collect()
    own_x.wait()

    def gw_own(dest):
        columns = pl.ds(pl.multiple_of(dest * RUN, RUN), RUN)
        return dot(xq[:, columns], gq[...], ((0,), (0,)))

    def gw_step(t):
        dests = (lax.rem(z + 4 - t, NZ), lax.rem(z + 4 + t, NZ))
        own = [gw_own(dest) for dest in dests]
        for way, half in ((0, 0), (1, 1), (0, 1), (1, 0)):
            if t == 0 and half != way:
                continue
            part = own[way][half * HALF : (half + 1) * HALF]
            index = way * 8 + t * 2 + half
            if t > 1 or (t == 1 and half == way):
                arrived(gwr.at[way, t - 1, half], M_GW + index - 2, z=ring_z[way])
                part = part + gwr[way, t - 1, half].astype(F32)
            gws[way, t, half] = part.astype(BF16)
            send(gws.at[way, t, half], gwr.at[way, t, half], M_GW + index, z=ring_z[way])

    def gw_end():
        own = gw_own(z)
        for half in (0, 1):
            part = own[half * HALF : (half + 1) * HALF]
            for way in (0, 1):
                arrived(gwr.at[way, 3, half], M_GW + way * 8 + 6 + half, z=ring_z[way])
                part = part + gwr[way, 3, half].astype(F32)
            gw_ref[half * HALF : (half + 1) * HALF, :] = part

    turn = lax.rem(x + NX - y, NX)

    def gi_rows(block, way, sub):
        return pl.ds(pl.multiple_of(block * RUN + way * HALF + sub * PIECE, PIECE), PIECE)

    def gi_product(d):
        block = pl.ds(pl.multiple_of(lax.rem(y + d, NY) * RUN, RUN), RUN)
        gia[block, :] = dot(gq[block, :], wq[pl.ds(mine, SLICE), :], ((1,), (1,))) + dot(
            gs[block, :], ws[...], ((1,), (1,))
        )

    def chain(slot):
        chain_step(slot, False)

    def chain_start():
        for i in range(8):
            chain_step(i, True)

    def chain_step(slot, start):
        for way in (0, 1):
            place = lax.rem(turn + 3, NX) if way == 0 else lax.rem(7 - turn, NX)
            to = lax.rem(x + 1, NX) if way == 0 else lax.rem(x + 3, NX)
            i = slot if start else slot - place

            @pl.when((place == 0) if start else ((place > 0) & (i >= 0) & (i < 8)))
            def _(way=way, place=place, to=to, i=i):
                block, sub = lax.rem(y + 1 + lax.div(i, 2), NY), lax.rem(i, 2)
                index = M_C + way * 8 + i
                own = gia[gi_rows(block, way, sub), :]

                if start:
                    gis[way, i] = own.astype(BF16)
                    message(gis.at[way, i], gir.at[way, i], index, x=to).start()
                    return
                arrived(gir.at[way, i], index, x=to)
                gis[way, pl.ds(i, 1)] = (own[None] + gir[way, pl.ds(i, 1)].astype(F32)).astype(BF16)

                @pl.when(place < 3)
                def _():
                    message(gis.at[way, i], gir.at[way, i], index, x=to).start()

                @pl.when((place == 3) & (i >= 6))
                def _():
                    gi_fin[gi_rows(0, way, sub), :] = gis[way, pl.ds(i, 1)][0]

                @pl.when((place == 3) & (i < 6))
                def _():
                    message(
                        gis.at[way, i], gi_fin.at[gi_rows(0, way, sub), :], index, M_D + way * 2 + sub, y=block
                    ).start()

    def product(start):
        def one_run(k, _):
            block = pl.ds(pl.multiple_of(k * RUN, RUN), RUN)
            part = dot(xq[block, pl.ds(start, SLICE)], wq[pl.ds(start, SLICE), :])
            acc[block, :] = part if start is mine else acc[block, :] + part
            return 0

        lax.fori_loop(0, NY, one_run, 0)

    near = (lax.rem(y + 1, NY), lax.rem(y + 3, NY))

    def v_part(run, half):
        return acc[pl.ds(pl.multiple_of(run * RUN + half * HALF, HALF), HALF), :]

    def v_out(part, way, k):
        vs[way, k] = part.astype(BF16)
        send(vs.at[way, k], vr.at[way, k], M_V + way * 3 + k, y=near[way])

    def v_in(way, k):
        arrived(vr.at[way, k], M_V + way * 3 + k, y=near[way])
        return vr[way, k].astype(F32)

    def v_send():
        for way in (0, 1):
            v_out(v_part(lax.rem(y + 2, NY), way), way, 0)
        for way in (0, 1):
            v_out(v_part(near[way], 1 - way), way, 1)

    def v_relay():
        for way in (0, 1):
            v_out(v_part(near[way], way) + v_in(way, 0), way, 2)

    def v_end():
        for half in (0, 1):
            total = v_part(y, half) + v_in(1 - half, 1) + v_in(half, 2)
            vals[half * HALF : (half + 1) * HALF, :] = total.astype(BF16)
        xs[...] = (vals[...].astype(F32) * shrink_x[...]).astype(BF16)

    product(mine)
    arrived(ws, M_WS, core=other)
    for d in range(NY):
        arrived(g_part(gs, lax.rem(y + NY - d, NY)), M_GS + d, core=other)
    for d in range(NY):
        gi_product(d)
    chain_start()
    for d in range(1, NY):
        arrived(x_part(lax.rem(y + NY - d, NY), other), M_XS + d - 1, core=other)
    product(theirs)
    v_send()
    gw_step(0)
    v_relay()
    chain(1)
    gw_step(1)
    chain(2)
    v_end()
    scan_pack(dot(xs[...], b_ref[...], ((0,), (0,))), f1)
    scan_out(f1, p1, M_FORE)
    chain(3)
    chain(4)
    gw_step(2)
    scan_rows(p1, f2, p2, M_FORE, up, False)
    chain(5)
    chain(6)

    mixed = jnp.zeros((RUN, RUN), F32)
    for pair in range(HEADS // 2):
        columns = slice(pair * 2 * DEPTH, (pair + 1) * 2 * DEPTH)
        part = vals[:, columns]
        for side in (0, 1):
            kept = jnp.where(low if side == 0 else ~low, part, jnp.zeros_like(part))
            mixed = mixed + dec[2 * pair + side] * dot(kept, dy_ref[:, columns], ((1,), (1,)))
    mixed = mixed.astype(BF16)
    grad_b = dot(mixed, c_ref[...]) + dot(xs[...], gin[...])
    grad_c = dot(mixed, b_ref[...], ((0,), (0,)))
    scan_back(p1, p2, f3, p3, M_FORE, up, False)
    gw_step(3)
    chain(7)
    chain(8)
    scan_in(p3, M_FORE, hin)
    grad_c = grad_c + dot(dg[...], hin[...])

    for k in range(NX * NC):
        share = slice(k * EIGHTH, (k + 1) * EIGHTH)
        part_send[k, :EIGHTH, :] = grad_b[share].astype(BF16)
        part_send[k, EIGHTH:, :] = grad_c[share].astype(BF16)
    for e in range(1, NX * NC):
        send(part_send.at[lax.rem(me + e, NX * NC)], part_recv.at[me], M_S + e - 1, **group_peer(e))
    part_recv[pl.ds(me, 1)] = part_send[pl.ds(me, 1)]
    chain(9)
    gw_end()
    for e in range(1, NX * NC):
        arrived(part_recv.at[lax.rem(me + NX * NC - e, NX * NC)], M_S + e - 1, **group_peer(e))
    total = part_recv[0].astype(F32)
    for k in range(1, NX * NC):
        total = total + part_recv[k].astype(F32)
    sums[pl.ds(me, 1)] = total.astype(BF16)[None]
    for e in range(1, NX * NC):
        send(sums.at[me], sums.at[me], M_S + 7 + e - 1, **group_peer(e))
    chain(10)
    for e in range(1, NX * NC):
        arrived(sums.at[lax.rem(me + NX * NC - e, NX * NC)], M_S + 7 + e - 1, **group_peer(e))
    for k in range(NX * NC):
        share = slice(k * EIGHTH, (k + 1) * EIGHTH)
        gb_ref[share, :] = sums[k, :EIGHTH, :].astype(F32)
        gc_ref[share, :] = sums[k, EIGHTH:, :].astype(F32)

    @pl.when(x != y)
    def _():
        for way in (0, 1):
            for sub in (0, 1):
                arrived(gi_fin.at[gi_rows(0, way, sub), :], M_D + way * 2 + sub, y=x)

    gi_ref[...] = gi_fin[...]
    for way in (0, 1):
        for i in range(8):
            sent = message(gis.at[way, i], gir.at[way, i], M_C + way * 8 + i, x=lax.rem(x + 1, NX))
            if i < 6:
                sent.wait_send()
            else:
                pl.when(x != y)(sent.wait_send)

    for copy in pending:
        copy.wait_send()


def hand_over(*refs):
    for source, result in zip(refs[:4], refs[4:], strict=True):
        result[...] = source[...]


def per_device(inputs, w_value, log_decay, b_proj, c_proj, grad_out):
    vmem = pl.BlockSpec(memory_space=pltpu.VMEM)

    def pair(count, *rest):
        return [pltpu.VMEM((count, *rest), BF16)] * 2

    def scan(rows):
        return [
            *pair(HEADS, rows, STATES),
            pltpu.VMEM((rows, STATES), BF16),
            pltpu.VMEM((NY, rows, STATES), BF16),
            *pair(HEADS, DEPTH, STATES),
        ]

    results = pl.pallas_call(
        kernel,
        out_shape=(
            jax.ShapeDtypeStruct((RUN, SLICE), BF16),
            jax.ShapeDtypeStruct((RUN, COLS), F32),
            jax.ShapeDtypeStruct((RUN, STATES), F32),
            jax.ShapeDtypeStruct((RUN, STATES), F32),
        ),
        in_specs=[pl.BlockSpec(memory_space=pl.ANY), vmem, vmem, vmem, vmem, vmem],
        out_specs=(vmem, vmem, vmem, vmem),
        scratch_shapes=[
            pltpu.VMEM((QUARTER, COLS), BF16),
            pltpu.VMEM((SLICE, COLS), BF16),
            pltpu.VMEM((NY * RUN, QUARTER), BF16),
            pltpu.VMEM((NY * RUN, COLS), BF16),
            pltpu.VMEM((NY * RUN, COLS), BF16),
            pltpu.VMEM((HEADS, RUN, RUN), F32),
            pltpu.VMEM((RUN, COLS), F32),
            pltpu.VMEM((RUN, COLS), F32),
            pltpu.VMEM((RUN, COLS), F32),
            pltpu.VMEM((RUN, COLS), BF16),
            pltpu.VMEM((RUN, COLS), BF16),
            pltpu.VMEM((RUN, COLS), BF16),
            pltpu.VMEM((HEADS * DEPTH, STATES), BF16),
            pltpu.VMEM((HEADS * DEPTH, STATES), BF16),
            *scan(PACK),
            *scan(DEPTH),
            pltpu.VMEM((NY * RUN, COLS), F32),
            pltpu.VMEM((NY * RUN, SLICE), F32),
            *pair(2, 3, HALF, COLS),
            *pair(2, 4, 2, HALF, COLS),
            *pair(2, 8, PIECE, SLICE),
            pltpu.VMEM((RUN, SLICE), BF16),
            *pair(NX * NC, 2 * EIGHTH, STATES),
            pltpu.VMEM((NX * NC, 2 * EIGHTH, STATES), BF16),
            pltpu.SemaphoreType.DMA((MESSAGES,)),
            pltpu.SemaphoreType.DMA((MESSAGES,)),
            pltpu.SemaphoreType.DMA,
        ],
        compiler_params=pltpu.CompilerParams(
            collective_id=0, has_side_effects=True, vmem_limit_bytes=56 * 2**20
        ),
        name="ssd_backward",
    )(inputs, w_value, log_decay.T, b_proj, c_proj, grad_out)
    return pl.pallas_call(
        hand_over,
        out_shape=tuple(jax.ShapeDtypeStruct(r.shape, r.dtype) for r in results),
        in_specs=[vmem] * 4,
        out_specs=(vmem,) * 4,
        name="hand_over",
    )(*results)


def solution(mesh):
    grid = Mesh(mesh.devices.reshape(NY, NZ, NX, NC), ("y", "z", "x", "core"))
    seq, head = ("y", "z"), ("x", "core")
    placed = (P(seq, None), P(seq, head), P(seq, head), P(seq, None), P(seq, None), P(seq, head))
    return jax.shard_map(
        per_device,
        mesh=grid,
        in_specs=placed,
        out_specs=(P(seq, head), P(seq, head), P(seq, None), P(seq, None)),
        check_vma=False,
    )
```

```python
import jax
import jax.numpy as jnp
from jax import lax
from jax.experimental import pallas as pl
from jax.experimental.pallas import tpu as pltpu
from jax.sharding import Mesh
from jax.sharding import PartitionSpec as P

NY, NZ, NX, NC = 4, 8, 4, 2
RUN = 256
HALF = RUN // 2
COLS = 512
HEADS = 8
DEPTH = 64
STATES = 128
QUARTER = 2048
SLICE = 1024
SUB = 256
EIGHTH = RUN // 8
PIECE = 64
PACK = DEPTH + 16
F32, BF16 = jnp.float32, jnp.bfloat16
HIGH = lax.Precision.HIGHEST

M_W = 0
M_WS = M_W + 16
M_X = M_WS + 1
M_XX = M_X + 3
M_XS = M_XX + 9
M_BACK = M_XS + 3
M_FORE = M_BACK + 17
M_G = M_FORE + 17
M_GS = M_G + 3
M_V = M_GS + 4
M_GW = M_V + 6
M_C = M_GW + 16
M_D = M_C + 16
M_S = M_D + 4
MESSAGES = M_S + 14


def dot(a, b, dims=((1,), (0,)), precision=None):
    return lax.dot_general(a, b, (dims, ((), ())), preferred_element_type=F32, precision=precision)


def kernel(
    x_hbm, w_ref, log_t_ref, b_ref, c_ref, dy_ref,
    gi_ref, gw_ref, gb_ref, gc_ref,
    wq, ws, xq, gq, gs, dec, gvi, grow_x, shrink_x, dg, xs, vals, gin, hin,
    b1, r1, b2, r2, b3, r3, f1, p1, f2, p2, f3, p3,
    acc, gia, vs, vr, gws, gwr, gis, gir, gi_fin,
    part_send, part_recv, sums,
    send_sem, recv_sem, local_sem,
):
    y, z = lax.axis_index("y"), lax.axis_index("z")
    x, core = lax.axis_index("x"), lax.axis_index("core")
    other = 1 - core
    pending = []

    def message(src, dst, index, at=None, **to):
        return pltpu.make_async_remote_copy(
            src_ref=src, dst_ref=dst, send_sem=send_sem.at[index], recv_sem=recv_sem.at[index if at is None else at],
            device_id=to, device_id_type=pl.DeviceIdType.MESH,
        )

    def send(src, dst, index, **to):
        copy = message(src, dst, index, **to)
        copy.start()
        pending.append(copy)

    def arrived(dst, index, **to):
        message(dst, dst, index, **to).wait_recv()

    def rows(ref, start, size):
        return ref.at[pl.ds(pl.multiple_of(start, size), size), :]

    me = x * NC + core

    def group_peer(e):
        to = lax.rem(me + e, NX * NC)
        return {"x": lax.div(to, NC), "core": lax.rem(to, NC)}

    barrier = pltpu.get_barrier_semaphore()
    for d in range(1, NZ):
        pl.semaphore_signal(barrier, inc=1, device_id={"z": lax.rem(z + d, NZ)}, device_id_type=pl.DeviceIdType.MESH)
    for d in range(1, NY):
        pl.semaphore_signal(barrier, inc=1, device_id={"y": lax.rem(y + d, NY)}, device_id_type=pl.DeviceIdType.MESH)
    for e in range(1, NX * NC):
        pl.semaphore_signal(barrier, inc=1, device_id=group_peer(e), device_id_type=pl.DeviceIdType.MESH)
    own_x = pltpu.make_async_copy(
        x_hbm.at[:, pl.ds(pl.multiple_of(y * QUARTER, QUARTER), QUARTER)], rows(xq, y * RUN, RUN), local_sem
    )
    own_x.start()
    wq[pl.ds(pl.multiple_of(z * RUN, RUN), RUN), :] = w_ref[...]

    one = lax.broadcasted_iota(jnp.int32, (RUN, RUN), 0)
    two = lax.broadcasted_iota(jnp.int32, (RUN, RUN), 1)
    logs = log_t_ref[...]
    cum = dot((one >= two).astype(F32), logs, ((1,), (1,)), HIGH)
    cum_t = dot(logs, (one <= two).astype(F32), precision=HIGH)
    head_of = lax.broadcasted_iota(jnp.int32, (HEADS, COLS), 1) // DEPTH
    spread = (lax.broadcasted_iota(jnp.int32, (HEADS, COLS), 0) == head_of).astype(F32)
    cum_x = dot(cum, spread, precision=HIGH)
    grow_x[...] = jnp.exp(cum_x)
    shrink_x[...] = jnp.exp(cum_x[RUN - 1 :, :] - cum_x)
    dg[...] = (dy_ref[...].astype(F32) * grow_x[...]).astype(BF16)

    first_rows = lax.broadcasted_iota(jnp.int32, (16, STATES), 0) < 8

    def two_terms(decay):
        decay = jnp.broadcast_to(decay, (16, STATES))
        high = decay.astype(BF16).astype(F32)
        return jnp.where(first_rows, high, decay - high).astype(BF16)

    def scan_pack(states, sent):
        for k in range(HEADS):
            sent[k, :DEPTH, :] = states[k * DEPTH : (k + 1) * DEPTH].astype(BF16)

    def scan_out(sent, got, base):
        for d in (4, 3, 5, 2, 6, 1, 7):
            to = lax.rem(z + d, NZ)
            send(sent.at[to], got.at[z], base + d - 1, z=to)
        got[pl.ds(z, 1)] = sent[pl.ds(z, 1)]

    scan_pack(dot(dg[...], c_ref[...], ((0,), (0,))), b1)
    for k in range(HEADS):
        b1[k, DEPTH:, :] = two_terms(jnp.exp(cum[RUN - 1 :, k : k + 1]))
    pl.semaphore_wait(barrier, NZ + NY + NX * NC - 3)
    scan_out(b1, r1, M_BACK)

    ring_z = (lax.rem(z + 1, NZ), lax.rem(z + NZ - 1, NZ))

    def w_part(shard, half):
        return rows(wq, shard * RUN + half * HALF, HALF)

    def w_send(way, hop, half):
        shard = lax.rem(z + NZ - (hop - 1), NZ) if way == 0 else lax.rem(z + (hop - 1), NZ)
        send(w_part(shard, half), w_part(shard, half), M_W + way * 8 + (hop - 1) * 2 + half, z=ring_z[way])

    def w_step(hop):
        for half in (0, 1):
            for way in (0, 1):
                if hop == NZ // 2 and half != way:
                    continue
                shard = lax.rem(z + NZ - hop, NZ) if way == 0 else lax.rem(z + hop, NZ)
                arrived(w_part(shard, half), M_W + way * 8 + (hop - 1) * 2 + half, z=ring_z[way])
                if hop < NZ // 2 - 1 or (hop == NZ // 2 - 1 and half == way):
                    w_send(way, hop + 1, half)

    for half in (0, 1):
        for way in (0, 1):
            w_send(way, 1, half)

    def x_part(row, col):
        return xq.at[
            pl.ds(pl.multiple_of(row * RUN, RUN), RUN), pl.ds(pl.multiple_of(col * SLICE, SLICE), SLICE)
        ]

    def x_piece(row, sub):
        return xq.at[
            pl.ds(pl.multiple_of(row * RUN, RUN), RUN), pl.ds(pl.multiple_of(core * SLICE + sub * SUB, SUB), SUB)
        ]

    for d in (2, 1, 3):
        to = lax.rem(y + d, NY)
        columns = pl.ds(pl.multiple_of(to * QUARTER + core * SLICE + x * SUB, SUB), SUB)
        send(x_hbm.at[:, columns], x_piece(y, x), M_X + d - 1, y=to)

    def x_relay():
        for d in (1, 3, 2):
            source = lax.rem(y + NY - d, NY)
            arrived(x_piece(source, x), M_X + d - 1, y=lax.rem(y + 1, NY))
            for e in (2, 1, 3):
                send(x_piece(source, x), x_piece(source, x), M_XX + (d - 1) * 3 + e - 1, x=lax.rem(x + e, NX))

    def x_collect():
        for d in (1, 3, 2):
            source = lax.rem(y + NY - d, NY)
            for e in (1, 2, 3):
                arrived(x_piece(source, lax.rem(x + NX - e, NX)), M_XX + (d - 1) * 3 + e - 1, x=lax.rem(x + 1, NX))
            send(x_part(source, core), x_part(source, core), M_XS + d - 1, core=other)

    def unpack(ref, decays, k):
        terms = decays[k, DEPTH:, :].astype(F32)
        return ref[k, :DEPTH, :].astype(F32), terms[:1, :] + terms[8:9, :]

    def scan_rows(got, sent, got_y, base, order, with_decay):
        for d in range(1, NZ):
            arrived(got.at[lax.rem(z + NZ - d, NZ)], base + d - 1, z=ring_z[0])
        carried, decays = jnp.zeros((DEPTH, STATES), F32), jnp.ones((1, STATES), F32)
        for k in order:
            state, decay = unpack(got, r1, k)
            carried = decay * carried + state
            decays = decays * decay
        sent[:DEPTH, :] = carried.astype(BF16)
        if with_decay:
            sent[DEPTH:, :] = two_terms(decays)
        for d in (2, 1, 3):
            to = lax.rem(y + d, NY)
            send(sent, got_y.at[y], base + 7 + d - 1, y=to)
        got_y[pl.ds(y, 1)] = sent[...][None]

    def scan_back(got, got_y, sent, got_z, base, order, reverse):
        for d in range(1, NY):
            arrived(got_y.at[lax.rem(y + NY - d, NY)], base + 7 + d - 1, y=lax.rem(y + 1, NY))
        carried = jnp.zeros((DEPTH, STATES), F32)
        for k in reversed(range(NY)) if reverse else range(NY):
            state, decay = unpack(got_y, r2, k)
            reached = (y < k) if reverse else (y > k)
            carried = jnp.where(reached, decay * carried + state, carried)
        for k in order:
            sent[k] = carried.astype(BF16)
            state, decay = unpack(got, r1, k)
            carried = decay * carried + state
        for d in (4, 3, 5, 2, 6, 1, 7):
            to = lax.rem(z + d, NZ)
            send(sent.at[to], got_z.at[z], base + 10 + d - 1, z=to)
        got_z[pl.ds(z, 1)] = sent[pl.ds(z, 1)]

    def scan_in(got_z, base, into):
        for d in range(1, NZ):
            arrived(got_z.at[lax.rem(z + NZ - d, NZ)], base + 10 + d - 1, z=ring_z[0])
        for k in range(HEADS):
            into[k * DEPTH : (k + 1) * DEPTH, :] = got_z[k]

    down, up = tuple(reversed(range(NZ))), tuple(range(NZ))

    scores = dot(b_ref[...], c_ref[...], ((1,), (1,)))
    low = lax.broadcasted_iota(jnp.int32, (RUN, 2 * DEPTH), 1) < DEPTH

    def within(pair):
        columns = slice(pair * 2 * DEPTH, (pair + 1) * 2 * DEPTH)
        part = dy_ref[:, columns]
        total = jnp.zeros((RUN, 2 * DEPTH), F32)
        for side in (0, 1):
            h = 2 * pair + side
            between = cum_t[h : h + 1, :] - cum[:, h : h + 1]
            decay = jnp.exp(jnp.where(two >= one, between, -1e30))
            dec[h] = decay
            kept = jnp.where(low if side == 0 else ~low, part, jnp.zeros_like(part))
            total = total + dot((decay * scores).astype(BF16), kept)
        gvi[:, columns] = total

    for pair in range(HEADS // 2):
        within(pair)
    scan_rows(r1, b2, r2, M_BACK, down, True)
    x_relay()
    scan_back(r1, r2, b3, r3, M_BACK, down, True)
    w_step(1)
    scan_in(r3, M_BACK, gin)

    def g_part(ref, row):
        return rows(ref, row * RUN, RUN)

    grad_values = gvi[...] + dot(b_ref[...], gin[...], ((1,), (1,))) * shrink_x[...]
    gq[pl.ds(pl.multiple_of(y * RUN, RUN), RUN), :] = grad_values.astype(BF16)
    for d in (2, 1, 3):
        send(g_part(gq, y), g_part(gq, y), M_G + d - 1, y=lax.rem(y + d, NY))
    send(g_part(gq, y), g_part(gs, y), M_GS, core=other)

    w_step(2)
    w_step(3)
    for d in (1, 3, 2):
        source = lax.rem(y + NY - d, NY)
        arrived(g_part(gq, source), M_G + d - 1, y=lax.rem(y + 1, NY))
        send(g_part(gq, source), g_part(gs, source), M_GS + d, core=other)
    w_step(4)
    theirs = pl.multiple_of(other * SLICE, SLICE)
    mine = pl.multiple_of(core * SLICE, SLICE)
    send(wq.at[pl.ds(theirs, SLICE), :], ws, M_WS, core=other)
    x_collect()
    own_x.wait()

    def gw_own(dest):
        columns = pl.ds(pl.multiple_of(dest * RUN, RUN), RUN)
        return dot(xq[:, columns], gq[...], ((0,), (0,)))

    def gw_step(t):
        dests = (lax.rem(z + 4 - t, NZ), lax.rem(z + 4 + t, NZ))
        own = [gw_own(dest) for dest in dests]
        for way, half in ((0, 0), (1, 1), (0, 1), (1, 0)):
            if t == 0 and half != way:
                continue
            part = own[way][half * HALF : (half + 1) * HALF]
            index = way * 8 + t * 2 + half
            if t > 1 or (t == 1 and half == way):
                arrived(gwr.at[way, t - 1, half], M_GW + index - 2, z=ring_z[way])
                part = part + gwr[way, t - 1, half].astype(F32)
            gws[way, t, half] = part.astype(BF16)
            send(gws.at[way, t, half], gwr.at[way, t, half], M_GW + index, z=ring_z[way])

    def gw_end():
        own = gw_own(z)
        for half in (0, 1):
            part = own[half * HALF : (half + 1) * HALF]
            for way in (0, 1):
                arrived(gwr.at[way, 3, half], M_GW + way * 8 + 6 + half, z=ring_z[way])
                part = part + gwr[way, 3, half].astype(F32)
            gw_ref[half * HALF : (half + 1) * HALF, :] = part

    turn = lax.rem(x + NX - y, NX)

    def gi_rows(block, way, sub):
        return pl.ds(pl.multiple_of(block * RUN + way * HALF + sub * PIECE, PIECE), PIECE)

    def gi_product(d):
        block = pl.ds(pl.multiple_of(lax.rem(y + d, NY) * RUN, RUN), RUN)
        gia[block, :] = dot(gq[block, :], wq[pl.ds(mine, SLICE), :], ((1,), (1,))) + dot(
            gs[block, :], ws[...], ((1,), (1,))
        )

    def chain(slot):
        chain_step(slot, False)

    def chain_start():
        for i in range(8):
            chain_step(i, True)

    def chain_step(slot, start):
        for way in (0, 1):
            place = lax.rem(turn + 3, NX) if way == 0 else lax.rem(7 - turn, NX)
            to = lax.rem(x + 1, NX) if way == 0 else lax.rem(x + 3, NX)
            i = slot if start else slot - place

            @pl.when((place == 0) if start else ((place > 0) & (i >= 0) & (i < 8)))
            def _(way=way, place=place, to=to, i=i):
                block, sub = lax.rem(y + 1 + lax.div(i, 2), NY), lax.rem(i, 2)
                index = M_C + way * 8 + i
                own = gia[gi_rows(block, way, sub), :]

                if start:
                    gis[way, i] = own.astype(BF16)
                    message(gis.at[way, i], gir.at[way, i], index, x=to).start()
                    return
                arrived(gir.at[way, i], index, x=to)
                gis[way, pl.ds(i, 1)] = (own[None] + gir[way, pl.ds(i, 1)].astype(F32)).astype(BF16)

                @pl.when(place < 3)
                def _():
                    message(gis.at[way, i], gir.at[way, i], index, x=to).start()

                @pl.when((place == 3) & (i >= 6))
                def _():
                    gi_fin[gi_rows(0, way, sub), :] = gis[way, pl.ds(i, 1)][0]

                @pl.when((place == 3) & (i < 6))
                def _():
                    message(
                        gis.at[way, i], gi_fin.at[gi_rows(0, way, sub), :], index, M_D + way * 2 + sub, y=block
                    ).start()

    def product(start):
        def one_run(k, _):
            block = pl.ds(pl.multiple_of(k * RUN, RUN), RUN)
            part = dot(xq[block, pl.ds(start, SLICE)], wq[pl.ds(start, SLICE), :])
            acc[block, :] = part if start is mine else acc[block, :] + part
            return 0

        lax.fori_loop(0, NY, one_run, 0)

    near = (lax.rem(y + 1, NY), lax.rem(y + 3, NY))

    def v_part(run, half):
        return acc[pl.ds(pl.multiple_of(run * RUN + half * HALF, HALF), HALF), :]

    def v_out(part, way, k):
        vs[way, k] = part.astype(BF16)
        send(vs.at[way, k], vr.at[way, k], M_V + way * 3 + k, y=near[way])

    def v_in(way, k):
        arrived(vr.at[way, k], M_V + way * 3 + k, y=near[way])
        return vr[way, k].astype(F32)

    def v_send():
        for way in (0, 1):
            v_out(v_part(lax.rem(y + 2, NY), way), way, 0)
        for way in (0, 1):
            v_out(v_part(near[way], 1 - way), way, 1)

    def v_relay():
        for way in (0, 1):
            v_out(v_part(near[way], way) + v_in(way, 0), way, 2)

    def v_end():
        for half in (0, 1):
            total = v_part(y, half) + v_in(1 - half, 1) + v_in(half, 2)
            vals[half * HALF : (half + 1) * HALF, :] = total.astype(BF16)
        xs[...] = (vals[...].astype(F32) * shrink_x[...]).astype(BF16)

    product(mine)
    arrived(ws, M_WS, core=other)
    for d in range(NY):
        arrived(g_part(gs, lax.rem(y + NY - d, NY)), M_GS + d, core=other)
    for d in range(NY):
        gi_product(d)
    chain_start()
    for d in range(1, NY):
        arrived(x_part(lax.rem(y + NY - d, NY), other), M_XS + d - 1, core=other)
    product(theirs)
    v_send()
    gw_step(0)
    v_relay()
    chain(1)
    gw_step(1)
    chain(2)
    v_end()
    scan_pack(dot(xs[...], b_ref[...], ((0,), (0,))), f1)
    scan_out(f1, p1, M_FORE)
    chain(3)
    chain(4)
    gw_step(2)
    scan_rows(p1, f2, p2, M_FORE, up, False)
    chain(5)
    chain(6)

    mixed = jnp.zeros((RUN, RUN), F32)
    for pair in range(HEADS // 2):
        columns = slice(pair * 2 * DEPTH, (pair + 1) * 2 * DEPTH)
        part = vals[:, columns]
        for side in (0, 1):
            kept = jnp.where(low if side == 0 else ~low, part, jnp.zeros_like(part))
            mixed = mixed + dec[2 * pair + side] * dot(kept, dy_ref[:, columns], ((1,), (1,)))
    mixed = mixed.astype(BF16)
    grad_b = dot(mixed, c_ref[...]) + dot(xs[...], gin[...])
    grad_c = dot(mixed, b_ref[...], ((0,), (0,)))
    scan_back(p1, p2, f3, p3, M_FORE, up, False)
    gw_step(3)
    chain(7)
    chain(8)
    scan_in(p3, M_FORE, hin)
    grad_c = grad_c + dot(dg[...], hin[...])

    for k in range(NX * NC):
        share = slice(k * EIGHTH, (k + 1) * EIGHTH)
        part_send[k, :EIGHTH, :] = grad_b[share].astype(BF16)
        part_send[k, EIGHTH:, :] = grad_c[share].astype(BF16)
    for e in range(1, NX * NC):
        send(part_send.at[lax.rem(me + e, NX * NC)], part_recv.at[me], M_S + e - 1, **group_peer(e))
    part_recv[pl.ds(me, 1)] = part_send[pl.ds(me, 1)]
    chain(9)
    gw_end()
    for e in range(1, NX * NC):
        arrived(part_recv.at[lax.rem(me + NX * NC - e, NX * NC)], M_S + e - 1, **group_peer(e))
    total = part_recv[0].astype(F32)
    for k in range(1, NX * NC):
        total = total + part_recv[k].astype(F32)
    sums[pl.ds(me, 1)] = total.astype(BF16)[None]
    for e in range(1, NX * NC):
        send(sums.at[me], sums.at[me], M_S + 7 + e - 1, **group_peer(e))
    chain(10)
    for e in range(1, NX * NC):
        arrived(sums.at[lax.rem(me + NX * NC - e, NX * NC)], M_S + 7 + e - 1, **group_peer(e))
    for k in range(NX * NC):
        share = slice(k * EIGHTH, (k + 1) * EIGHTH)
        gb_ref[share, :] = sums[k, :EIGHTH, :].astype(F32)
        gc_ref[share, :] = sums[k, EIGHTH:, :].astype(F32)

    @pl.when(x != y)
    def _():
        for way in (0, 1):
            for sub in (0, 1):
                arrived(gi_fin.at[gi_rows(0, way, sub), :], M_D + way * 2 + sub, y=x)

    gi_ref[...] = gi_fin[...]
    for way in (0, 1):
        for i in range(8):
            sent = message(gis.at[way, i], gir.at[way, i], M_C + way * 8 + i, x=lax.rem(x + 1, NX))
            if i < 6:
                sent.wait_send()
            else:
                pl.when(x != y)(sent.wait_send)

    for copy in pending:
        copy.wait_send()


def hand_over(*refs):
    for source, result in zip(refs[:4], refs[4:], strict=True):
        result[...] = source[...]


def per_device(inputs, w_value, log_decay, b_proj, c_proj, grad_out):
    vmem = pl.BlockSpec(memory_space=pltpu.VMEM)

    def pair(count, *rest):
        return [pltpu.VMEM((count, *rest), BF16)] * 2

    def scan(rows):
        return [
            *pair(HEADS, rows, STATES),
            pltpu.VMEM((rows, STATES), BF16),
            pltpu.VMEM((NY, rows, STATES), BF16),
            *pair(HEADS, DEPTH, STATES),
        ]

    results = pl.pallas_call(
        kernel,
        out_shape=(
            jax.ShapeDtypeStruct((RUN, SLICE), BF16),
            jax.ShapeDtypeStruct((RUN, COLS), F32),
            jax.ShapeDtypeStruct((RUN, STATES), F32),
            jax.ShapeDtypeStruct((RUN, STATES), F32),
        ),
        in_specs=[pl.BlockSpec(memory_space=pl.ANY), vmem, vmem, vmem, vmem, vmem],
        out_specs=(vmem, vmem, vmem, vmem),
        scratch_shapes=[
            pltpu.VMEM((QUARTER, COLS), BF16),
            pltpu.VMEM((SLICE, COLS), BF16),
            pltpu.VMEM((NY * RUN, QUARTER), BF16),
            pltpu.VMEM((NY * RUN, COLS), BF16),
            pltpu.VMEM((NY * RUN, COLS), BF16),
            pltpu.VMEM((HEADS, RUN, RUN), F32),
            pltpu.VMEM((RUN, COLS), F32),
            pltpu.VMEM((RUN, COLS), F32),
            pltpu.VMEM((RUN, COLS), F32),
            pltpu.VMEM((RUN, COLS), BF16),
            pltpu.VMEM((RUN, COLS), BF16),
            pltpu.VMEM((RUN, COLS), BF16),
            pltpu.VMEM((HEADS * DEPTH, STATES), BF16),
            pltpu.VMEM((HEADS * DEPTH, STATES), BF16),
            *scan(PACK),
            *scan(DEPTH),
            pltpu.VMEM((NY * RUN, COLS), F32),
            pltpu.VMEM((NY * RUN, SLICE), F32),
            *pair(2, 3, HALF, COLS),
            *pair(2, 4, 2, HALF, COLS),
            *pair(2, 8, PIECE, SLICE),
            pltpu.VMEM((RUN, SLICE), BF16),
            *pair(NX * NC, 2 * EIGHTH, STATES),
            pltpu.VMEM((NX * NC, 2 * EIGHTH, STATES), BF16),
            pltpu.SemaphoreType.DMA((MESSAGES,)),
            pltpu.SemaphoreType.DMA((MESSAGES,)),
            pltpu.SemaphoreType.DMA,
        ],
        compiler_params=pltpu.CompilerParams(
            collective_id=0, has_side_effects=True, vmem_limit_bytes=56 * 2**20
        ),
        name="ssd_backward",
    )(inputs, w_value, log_decay.T, b_proj, c_proj, grad_out)
    return pl.pallas_call(
        hand_over,
        out_shape=tuple(jax.ShapeDtypeStruct(r.shape, r.dtype) for r in results),
        in_specs=[vmem] * 4,
        out_specs=(vmem,) * 4,
        name="hand_over",
    )(*results)


def solution(mesh):
    grid = Mesh(mesh.devices.reshape(NY, NZ, NX, NC), ("y", "z", "x", "core"))
    seq, head = ("y", "z"), ("x", "core")
    placed = (P(seq, None), P(seq, head), P(seq, head), P(seq, None), P(seq, None), P(seq, head))
    return jax.shard_map(
        per_device,
        mesh=grid,
        in_specs=placed,
        out_specs=(P(seq, head), P(seq, head), P(seq, None), P(seq, None)),
        check_vma=False,
    )
```
